512 devices in a mesh: pair: 64 (over y, z), tm: 8 (over x, core).
Axes of the slice: x: 4, y: 4, z: 16, core: 2. Of those that a mesh axis runs over, the one named last changes fastest.
Arguments:
- traces: bfloat16 [16, 2048, 8192], P('tm', None, 'pair'), may hold values from -6 to 6
- source_list: int32 [64, 8], replicated, may hold values from 0 to 63
- source_count: int32 [64], replicated, may hold values from 1 to 8, 320 in all
- receiver_start: int32 [64], replicated, may hold values from 65 to 127
- segment_slot: int32 [16], replicated, may hold values from 0 to 1, as said below
Outputs:
- stacks: bfloat16 [8, 2, 512, 64, 128], P('tm', None, 'pair')
The draws below stay inside these ranges and needn't reach their ends.
Inputs may be any that keep to these rules, and one draw needn't show every extreme that they name: `source_list`: block index of a virtual source. The live slots of owner p are its first source_count[p] slots. `receiver_start`: every receiver window reaches into the next block. `segment_slot`: every stack receives exactly 8 segments.
All inputs are finite; a program needn't handle non-finite values.
Results may differ from the reference program's by a relative error of at most 0.0067.
Values may be sent and summed in bfloat16 or wider, within the bound.
No kernel may reach another device: no remote copies, remote signals or barrier semaphores. Data moves between devices by JAX's collectives and lax.ppermute only.
A program may use at most 64 MiB of HBM per device.

```python
import math
import jax
import jax.numpy as jnp
import numpy as np
from jax import lax

CH = 128
SAMPLES = 2048
NF = 512
BAND = 32
K = 8
R_CH = 64
LAGS = 8
SLOTS = 2
F0 = 64
SEGS = 16
CHANNELS = 8192
N_PAIR = 64


def draw_segment_slot(key, part):
    order = jax.random.permutation(jax.random.fold_in(key, 7), SEGS)
    return (order % SLOTS).astype(jnp.int32)


def place_ends(array, own_key, smallest, largest):
    longest = array.shape.index(max(array.shape))
    spots = []
    for shift in (0, 1):
        where = [jax.random.randint(jax.random.fold_in(own_key, axis), (), 0, length) for axis, length in enumerate(array.shape)]
        where[longest] = (where[longest] + shift) % array.shape[longest]
        spots.append(tuple(where))
    return array.at[spots[0]].set(smallest).at[spots[1]].set(largest)


def levels(stream_key, extent, split, smallest, high):
    factor_of = 1.0
    for position, shards_of in split:
        steps = jax.random.uniform(jax.random.fold_in(jax.random.fold_in(stream_key, 6), position), (shards_of,), jnp.float32, smallest / len(split), high / len(split))
        factor_of = factor_of * jnp.repeat(jnp.exp(steps), extent[position] // shards_of).reshape((-1,) + (1,) * (len(extent) - 1 - position))
    return factor_of


def cumulative_ranks(number_of, lean):
    loads = [(1 << 20) // math.isqrt(rank ** lean) + 1 for rank in range(1, number_of + 1)]
    width = 1 + sum(loads) // (1 << 30)
    return np.cumsum(np.array([max(1, weight // width) for weight in loads]))


def ranked(key, extent, amount, lean):
    table = cumulative_ranks(amount, lean)
    pick = jax.random.randint(jax.random.fold_in(key, 1), extent, 0, int(table[amount - 1]))
    rank = jnp.searchsorted(jnp.asarray(table, jnp.int32), pick, side="right")
    return jax.random.permutation(jax.random.fold_in(key, 2), amount)[rank].astype(jnp.int32)


def split_up(number_of, total, reach, slope):
    weights = [(1 << 20) // math.isqrt(standing ** slope) + 1 for standing in range(2, number_of + 1)]
    spare, holding = total - reach - (number_of - 1), [1] * (number_of - 1)
    while spare > 0:
        free = [i for i in range(number_of - 1) if holding[i] < reach]
        pool, remaining = sum([weights[i] for i in free]), spare
        for i in free:
            more = min(reach - holding[i], max(1, remaining * weights[i] // pool), spare)
            holding[i] = holding[i] + more
            spare = spare - more
    return np.array([reach] + holding)


def uneven(rng, count, total, reach, slope):
    if count == 2:
        one = jax.random.randint(rng, (), max(1, total - reach), min(reach, total - 1) + 1)
        return jnp.stack([one, total - one])
    lengths = jnp.asarray(split_up(count, total, reach, slope), jnp.int32)
    pairs = (count - 1) // 2
    giver, receiver = lengths[1:1 + 2 * pairs:2], lengths[2:2 + 2 * pairs:2]
    slack = jnp.minimum(giver - 1, reach - receiver)
    moved = jax.random.randint(jax.random.fold_in(rng, 1), (pairs,), 0, 1 << 20) % (slack + 1)
    lengths = lengths.at[1:1 + 2 * pairs:2].set(giver - moved).at[2:2 + 2 * pairs:2].set(receiver + moved)
    return lengths[jax.random.permutation(jax.random.fold_in(rng, 2), count)]


def bell_draw(stream_key, dims, scale, most, pieces=(), held_as=jnp.bfloat16):
    entries = jax.random.normal(stream_key, dims, jnp.float32) * scale
    if len(pieces) > 0:
        entries = levels(stream_key, dims, pieces, -0.22, 0.18) * entries
    return jnp.clip(entries, min=-most, max=most).astype(held_as)


def setup_inputs(seed: int = 0) -> dict:
    streams_of = jax.random.split(jax.random.key(seed), 6)
    traces = bell_draw(streams_of[0], (SEGS, SAMPLES, CHANNELS), 1.0, 6.0, ((0, 8), (2, 64)))
    source_list = place_ends(ranked(streams_of[1], (N_PAIR, K), N_PAIR, 2), jax.random.fold_in(streams_of[1], 3), 0, N_PAIR - 1).astype(jnp.int32)
    source_count = uneven(streams_of[2], N_PAIR, N_PAIR * K * 5 // 8, K, 2).astype(jnp.int32)
    receiver_start = place_ends(jax.random.randint(streams_of[3], (N_PAIR,), CH - R_CH + 1, CH), jax.random.fold_in(streams_of[3], 1), CH - R_CH + 1, CH - 1).astype(jnp.int32)
    segment_slot = draw_segment_slot(jax.random.fold_in(streams_of[5], 71), 0)
    return {"traces": traces, "source_list": source_list, "source_count": source_count, "receiver_start": receiver_start, "segment_slot": segment_slot}


whiten_eps = 1e-06

def transform_table():
    bins = F0 + jnp.arange(NF, dtype=jnp.int32)
    sample_steps = jnp.arange(SAMPLES, dtype=jnp.int32)
    phase = bins[:, None] * sample_steps[None, :] % SAMPLES
    angle = 2.0 * jnp.pi / SAMPLES * phase.astype(jnp.float32)
    table = jnp.concatenate([jnp.cos(angle), -jnp.sin(angle)], axis=0)
    return table.astype(jnp.bfloat16)

def whiten_block(block_traces):
    table = transform_table().astype(jnp.float32)
    spectra = jnp.einsum('fn,snc->sfc', table, block_traces.astype(jnp.float32))
    seg_count = block_traces.shape[0]
    grouped = spectra.reshape(seg_count, 2, NF // BAND, BAND, CH)
    band_power = lax.optimization_barrier(jnp.mean(grouped * grouped, axis=(1, 3), keepdims=True))
    whitened = grouped / jnp.sqrt(band_power + whiten_eps)
    return whitened.reshape(seg_count, 2, NF, CH).astype(jnp.bfloat16)

def lag_kernel(window, slot_ids):
    seg_count = window.shape[0]
    bins = F0 + jnp.arange(NF, dtype=jnp.int32)
    lag_steps = jnp.arange(LAGS, dtype=jnp.int32) - LAGS // 2
    phase = lag_steps[:, None] * bins[None, :] % SAMPLES
    angle = 2.0 * jnp.pi / SAMPLES * phase.astype(jnp.float32)
    lag_cos = jnp.cos(angle)[:, None, None, :]
    lag_sin = jnp.sin(angle)[:, None, None, :]
    window_t = jnp.transpose(window.astype(jnp.float32), (3, 0, 1, 2))
    recv_real = window_t[:, :, 0][None]
    recv_imag = window_t[:, :, 1][None]
    for_real = lag_cos * recv_real + lag_sin * recv_imag
    for_imag = lag_cos * recv_imag - lag_sin * recv_real
    both = jnp.stack([for_real, for_imag], axis=3)
    onehot = (slot_ids[None, :] == jnp.arange(SLOTS, dtype=jnp.int32)[:, None]).astype(jnp.float32)
    norm_factor = (2.0 * NF * SEGS / SLOTS) ** (-0.5)
    weighted = both[:, None] * onehot[None, :, None, :, None, None] * norm_factor
    return weighted.reshape(LAGS, SLOTS, R_CH, seg_count * 2 * NF).astype(jnp.bfloat16)

def reference(traces, source_list, source_count, receiver_start, segment_slot):
    blocked = jnp.transpose(traces.reshape(SEGS, SAMPLES, N_PAIR, CH), (2, 0, 1, 3))
    whitened_all = lax.map(whiten_block, blocked)

    def one_owner(owner):
        own = whitened_all[owner]
        following = whitened_all[jnp.minimum(owner + 1, N_PAIR - 1)]
        beyond = jnp.where(owner + 1 < N_PAIR, following, jnp.zeros_like(following))
        joined = jnp.concatenate([own, beyond], axis=3)
        window = lax.dynamic_slice_in_dim(joined, receiver_start[owner].astype(jnp.int32), R_CH, 3)
        kernel = lag_kernel(window, segment_slot)
        live_slots = (jnp.arange(K, dtype=jnp.int32) < source_count[owner]).astype(jnp.bfloat16)
        sources = whitened_all[source_list[owner]] * live_slots[:, None, None, None, None]
        sources = sources.reshape(K, SEGS * 2 * NF, CH)
        correlation = jnp.einsum('lqjc,kci->lqkji', kernel.astype(jnp.float32), sources.astype(jnp.float32))
        return correlation.astype(jnp.bfloat16)
    stacked = lax.map(one_owner, jnp.arange(N_PAIR, dtype=jnp.int32))
    stacked = jnp.transpose(stacked, (1, 2, 0, 3, 4, 5))
    return stacked.reshape(LAGS, SLOTS, N_PAIR * K, R_CH, CH)
```

```python
import jax
import jax.numpy as jnp
import numpy as np
from jax import lax
from jax.experimental import pallas as pl
from jax.experimental.pallas import tpu as pltpu
from jax.sharding import Mesh, PartitionSpec as P

CH = 128
SAMPLES = 2048
NF = 512
BAND = 32
K = 8
R_CH = 64
LAGS = 8
SLOTS = 2
F0 = 64
SEGS = 16
NY, NZ, NX, NC = 4, 16, 4, 2
SEG = 2
CQ = CH // NY
FB = 128
NB = NF // FB
KF = 2 * NF
EPS = 1e-06
NORM = np.float32((2.0 * NF * SEGS / SLOTS) ** (-0.5))
BF = jnp.bfloat16
F32 = jnp.float32
VMEM = 48 * 1024 * 1024


def transform_table():
    bins = F0 + np.arange(NF, dtype=np.int64)
    phase = (bins[:, None] * np.arange(SAMPLES // 2, dtype=np.int64)[None, :]) % SAMPLES
    steps = np.arange(SAMPLES, dtype=np.float32) * np.float32(2.0 * np.pi / SAMPLES)
    cos = np.cos(steps)[phase]
    sin = -np.sin(steps)[phase]
    return np.stack([cos, sin], axis=0).astype(jnp.bfloat16)


def lag_tables():
    bins = F0 + np.arange(NF, dtype=np.int64)
    lags = np.arange(LAGS, dtype=np.int64) - LAGS // 2
    phase = (lags[:, None] * bins[None, :]) % SAMPLES
    angle = phase.astype(np.float32) * np.float32(2.0 * np.pi / SAMPLES)
    return np.stack([np.cos(angle), np.sin(angle)], axis=0).astype(np.float32)


def whiten_kernel(traces_ref, table_ref, split_ref, low_ref, high_ref):
    half = SAMPLES // 2
    table = table_ref[...].reshape(2 * FB, half)
    early = jnp.concatenate([traces_ref[s, :half] for s in range(SEG)], axis=1)
    late = jnp.concatenate([traces_ref[s, half:] for s in range(SEG)], axis=1)
    early = jnp.dot(table, early, preferred_element_type=F32)
    late = jnp.dot(table, late, preferred_element_type=F32)
    odd = lax.broadcasted_iota(jnp.int32, late.shape, 0) % 2 == 1
    spectra = early + jnp.where(odd, -late, late)
    grouped = spectra.reshape(2, FB // BAND, BAND, SEG * CH)
    power = jnp.sum(grouped * grouped, axis=(0, 2)) * (1.0 / (2 * BAND))
    scale = 1.0 / jnp.sqrt(power + EPS)
    whitened = grouped * scale[None, :, None, :]
    flipped = whitened.reshape(2 * FB, SEG * CH).T.astype(BF)
    for s in range(SEG):
        low_ref[s] = flipped[s * CH : s * CH + CH // 2]
        high_ref[s] = flipped[s * CH + CH // 2 : (s + 1) * CH]
        for y in range(NY):
            split_ref[y, s] = flipped[s * CH + y * CQ : s * CH + (y + 1) * CQ]


def whiten(traces, table):
    half = jax.ShapeDtypeStruct((SEG, CH // 2, KF), BF)
    half_spec = pl.BlockSpec((SEG, CH // 2, 2 * FB), lambda g: (0, 0, g))
    return pl.pallas_call(
        whiten_kernel,
        grid=(NB,),
        in_specs=[
            pl.BlockSpec((SEG, SAMPLES, CH), lambda g: (0, 0, 0)),
            pl.BlockSpec((2, FB, SAMPLES // 2), lambda g: (0, g, 0)),
        ],
        out_specs=[
            pl.BlockSpec((NY, SEG, CQ, 2 * FB), lambda g: (0, 0, 0, g)),
            half_spec,
            half_spec,
        ],
        out_shape=[jax.ShapeDtypeStruct((NY, SEG, CQ, KF), BF), half, half],
        compiler_params=pltpu.CompilerParams(vmem_limit_bytes=VMEM),
        name="whiten",
    )(traces, table)


def lag_kernel_body(window_ref, lag_ref, out_ref):
    for b in range(NB):
        at = b * 2 * FB
        real = window_ref[0, 0, :, at : at + FB].astype(F32)
        imag = window_ref[0, 0, :, at + FB : at + 2 * FB].astype(F32)
        for l in range(LAGS):
            cos = lag_ref[0, l : l + 1, b * FB : (b + 1) * FB]
            sin = lag_ref[1, l : l + 1, b * FB : (b + 1) * FB]
            for_real = (cos * real + sin * imag) * NORM
            for_imag = (cos * imag - sin * real) * NORM
            out_ref[0, 0, l, :, at : at + FB] = for_real.astype(BF)
            out_ref[0, 0, l, :, at + FB : at + 2 * FB] = for_imag.astype(BF)


def lag_kernels(windows, lags):
    return pl.pallas_call(
        lag_kernel_body,
        grid=(NY, SEG),
        in_specs=[
            pl.BlockSpec((1, 1, R_CH, KF), lambda o, s: (o, s, 0, 0)),
            pl.BlockSpec((2, LAGS, NF), lambda o, s: (0, 0, 0)),
        ],
        out_specs=pl.BlockSpec((1, 1, LAGS, R_CH, KF), lambda o, s: (o, s, 0, 0, 0)),
        out_shape=jax.ShapeDtypeStruct((NY, SEG, LAGS, R_CH, KF), BF),
        compiler_params=pltpu.CompilerParams(vmem_limit_bytes=VMEM),
        name="lag_kernels",
    )(windows, lags)


def correlate_body(info_ref, kernel_ref, *refs):
    sources, out_ref = refs[:K], refs[K]
    o = pl.program_id(0)
    count = info_ref[64 + o]
    lane = lax.broadcasted_iota(jnp.int32, (1, K * CQ), 1)
    live = (lane < count * CQ).astype(F32)
    sums = []
    for s in range(SEG):
        left = kernel_ref[0, s].reshape(LAGS * R_CH, KF)
        right = jnp.concatenate([ref[0, 0, s] for ref in sources], axis=0)
        sums.append(lax.dot_general(left, right, (((1,), (1,)), ((), ())), preferred_element_type=F32))
    for q in range(SLOTS):
        total = 0.0
        for s in range(SEG):
            total = total + sums[s] * (live * (info_ref[68 + s] == q).astype(F32))
        out_ref[0, :, q] = total.reshape(LAGS, R_CH, K * CQ).astype(BF)


def correlate(info, kernels, gathered):
    def source_map(k):
        return lambda o, info: (info[o * K + k], info[32 + o * K + k], 0, 0, 0)

    return pl.pallas_call(
        correlate_body,
        grid_spec=pltpu.PrefetchScalarGridSpec(
            num_scalar_prefetch=1,
            grid=(NY,),
            in_specs=[
                pl.BlockSpec(
                    (1, SEG, LAGS, R_CH, KF),
                    lambda o, info: (lax.rem(info[70] + NY - o, NY), 0, 0, 0, 0),
                )
            ]
            + [pl.BlockSpec((1, 1, SEG, CQ, KF), source_map(k)) for k in range(K)],
            out_specs=pl.BlockSpec((1, LAGS, SLOTS, R_CH, K * CQ), lambda o, info: (o, 0, 0, 0, 0)),
        ),
        out_shape=jax.ShapeDtypeStruct((NY, LAGS, SLOTS, R_CH, K * CQ), BF),
        compiler_params=pltpu.CompilerParams(vmem_limit_bytes=VMEM),
        name="correlate",
    )(info, kernels, *([gathered] * K))


def finish_body(parts_ref, out_ref):
    n = NX * NC
    quarter = []
    for y in range(NY):
        total = parts_ref[y * n, 0].astype(F32)
        for t in range(1, n):
            total = total + parts_ref[y * n + t, 0].astype(F32)
        quarter.append(total)
    for k in range(K):
        row = jnp.concatenate([v[:, k * CQ : (k + 1) * CQ] for v in quarter], axis=1)
        out_ref[0, 0, k] = row.astype(BF)


def finish(parts):
    return pl.pallas_call(
        finish_body,
        grid=(SLOTS,),
        in_specs=[pl.BlockSpec((NY * NX * NC, 1, R_CH, K * CQ), lambda q: (0, q, 0, 0))],
        out_specs=pl.BlockSpec((1, 1, K, R_CH, CH), lambda q: (0, q, 0, 0, 0)),
        out_shape=jax.ShapeDtypeStruct((1, SLOTS, K, R_CH, CH), BF),
        compiler_params=pltpu.CompilerParams(vmem_limit_bytes=VMEM),
        name="finish",
    )(parts)


def body(traces, source_list, source_count, receiver_start, segment_slot):
    y = lax.axis_index("y")
    z = lax.axis_index("z")
    t = lax.axis_index(("x", "c"))
    table = jnp.asarray(transform_table())
    lags = jnp.asarray(lag_tables())
    split, low, high = whiten(traces, table)
    crossed = lax.all_to_all(split, "y", 0, 0)
    gathered = lax.all_gather(crossed, "z", axis=0, tiled=False)

    low, high, _ = lax.optimization_barrier((low, high, crossed))
    pairs = NY * NZ
    following = lax.ppermute(low, ("y", "z"), [(p, p - 1) for p in range(1, pairs)])
    joined = jnp.concatenate([high, following], axis=1)
    offset = lax.dynamic_index_in_dim(receiver_start, y * NZ + z, keepdims=False) - CH // 2
    window = lax.dynamic_slice_in_dim(joined, offset, R_CH, 1)
    windows = jnp.stack(
        [window] + [lax.ppermute(window, "y", [(i, (i + d) % NY) for i in range(NY)]) for d in range(1, NY)]
    )
    kernels = lag_kernels(windows, lags)

    lists = lax.dynamic_index_in_dim(source_list.reshape(NY, NZ, K), z, 1, keepdims=False).reshape(-1)
    counts = lax.dynamic_index_in_dim(source_count.reshape(NY, NZ), z, 1, keepdims=False)
    slots = lax.dynamic_slice_in_dim(segment_slot, t * SEG, SEG, 0)
    info = jnp.concatenate([lists % NZ, lists // NZ, counts, slots, y[None].astype(jnp.int32)])
    sums = correlate(info, kernels, gathered)
    parts = sums.reshape(NY * LAGS, SLOTS, R_CH, K * CQ)
    parts = lax.all_to_all(parts, ("y", "x", "c"), 0, 0)
    return finish(parts)


def solution(mesh):
    grid = Mesh(mesh.devices.reshape(NY, NZ, NX, NC), ("y", "z", "x", "c"))
    tm, pair = ("x", "c"), ("y", "z")
    return jax.shard_map(
        body,
        mesh=grid,
        in_specs=(P(tm, None, pair), P(), P(), P(), P()),
        out_specs=P(tm, None, pair, None, None),
        check_vma=False,
    )
```

```python
import jax
import jax.numpy as jnp
import numpy as np
from jax import lax
from jax.experimental import pallas as pl
from jax.experimental.pallas import tpu as pltpu
from jax.sharding import Mesh, PartitionSpec as P

CH = 128
SAMPLES = 2048
NF = 512
BAND = 32
K = 8
R_CH = 64
LAGS = 8
SLOTS = 2
F0 = 64
SEGS = 16
NY, NZ, NX, NC = 4, 16, 4, 2
G = 4
NH = NZ // G
NP = NY * G
SEG = 2
CQ = CH // NP
W = SLOTS * K * CQ
FB = 128
NB = NF // FB
KF = 2 * NF
EPS = 1e-06
NORM = np.float32((2.0 * NF * SEGS / SLOTS) ** (-0.5))
BF = jnp.bfloat16
F32 = jnp.float32
VMEM = 48 * 1024 * 1024


def transform_table():
    bins = F0 + np.arange(NF, dtype=np.int64)
    phase = (bins[:, None] * np.arange(SAMPLES // 2, dtype=np.int64)[None, :]) % SAMPLES
    steps = np.arange(SAMPLES, dtype=np.float32) * np.float32(2.0 * np.pi / SAMPLES)
    cos = np.cos(steps)[phase]
    sin = -np.sin(steps)[phase]
    return np.stack([cos, sin], axis=0).astype(jnp.bfloat16)


def lag_tables():
    bins = F0 + np.arange(NF, dtype=np.int64)
    lags = np.arange(LAGS, dtype=np.int64) - LAGS // 2
    phase = (lags[:, None] * bins[None, :]) % SAMPLES
    angle = phase.astype(np.float32) * np.float32(2.0 * np.pi / SAMPLES)
    return np.stack([np.cos(angle), np.sin(angle)], axis=0).astype(np.float32)


def whiten_kernel(traces_ref, table_ref, split_ref, low_ref, high_ref):
    half = SAMPLES // 2
    table = table_ref[...].reshape(2 * FB, half)
    early = jnp.concatenate([traces_ref[s, :half] for s in range(SEG)], axis=1)
    late = jnp.concatenate([traces_ref[s, half:] for s in range(SEG)], axis=1)
    early = jnp.dot(table, early, preferred_element_type=F32)
    late = jnp.dot(table, late, preferred_element_type=F32)
    odd = lax.broadcasted_iota(jnp.int32, late.shape, 0) % 2 == 1
    spectra = early + jnp.where(odd, -late, late)
    grouped = spectra.reshape(2, FB // BAND, BAND, SEG * CH)
    power = jnp.sum(grouped * grouped, axis=(0, 2)) * (1.0 / (2 * BAND))
    scale = 1.0 / jnp.sqrt(power + EPS)
    whitened = grouped * scale[None, :, None, :]
    flipped = whitened.reshape(2 * FB, SEG * CH).T
    for s in range(SEG):
        low_ref[s] = flipped[s * CH : s * CH + CH // 2].astype(BF)
        high_ref[s] = flipped[s * CH + CH // 2 : (s + 1) * CH].astype(BF)
        for r in range(NP):
            split_ref[r, s] = flipped[s * CH + r * CQ : s * CH + (r + 1) * CQ].astype(BF)


def whiten(traces, table):
    half = jax.ShapeDtypeStruct((SEG, CH // 2, KF), BF)
    half_spec = pl.BlockSpec((SEG, CH // 2, 2 * FB), lambda g: (0, 0, g))
    return pl.pallas_call(
        whiten_kernel,
        grid=(NB,),
        in_specs=[
            pl.BlockSpec((SEG, SAMPLES, CH), lambda g: (0, 0, 0)),
            pl.BlockSpec((2, FB, SAMPLES // 2), lambda g: (0, g, 0)),
        ],
        out_specs=[
            pl.BlockSpec((NP, SEG, CQ, 2 * FB), lambda g: (0, 0, 0, g)),
            half_spec,
            half_spec,
        ],
        out_shape=[jax.ShapeDtypeStruct((NP, SEG, CQ, KF), BF), half, half],
        compiler_params=pltpu.CompilerParams(vmem_limit_bytes=VMEM),
        name="whiten",
    )(traces, table)


def lag_kernel_body(window_ref, lag_ref, *refs):
    out_ref = refs[-1]
    for b in range(NB):
        at = b * 2 * FB
        real = window_ref[0, 0, :, at : at + FB].astype(F32)
        imag = window_ref[0, 0, :, at + FB : at + 2 * FB].astype(F32)
        for l in range(LAGS):
            cos = lag_ref[0, l : l + 1, b * FB : (b + 1) * FB]
            sin = lag_ref[1, l : l + 1, b * FB : (b + 1) * FB]
            for_real = (cos * real + sin * imag) * NORM
            for_imag = (cos * imag - sin * real) * NORM
            out_ref[0, 0, l, :, at : at + FB] = for_real.astype(BF)
            out_ref[0, 0, l, :, at + FB : at + 2 * FB] = for_imag.astype(BF)


def lag_kernels(d, windows, lags, kernels):
    earlier = [] if kernels is None else [kernels]
    return pl.pallas_call(
        lag_kernel_body,
        grid=(G, SEG),
        in_specs=[
            pl.BlockSpec((1, 1, R_CH, KF), lambda o, s: (o, s, 0, 0)),
            pl.BlockSpec((2, LAGS, NF), lambda o, s: (0, 0, 0)),
        ]
        + [pl.BlockSpec(memory_space=pl.ANY)] * len(earlier),
        out_specs=pl.BlockSpec((1, 1, LAGS, R_CH, KF), lambda o, s: (d * G + o, s, 0, 0, 0)),
        out_shape=jax.ShapeDtypeStruct((NP, SEG, LAGS, R_CH, KF), BF),
        input_output_aliases={2: 0} if earlier else {},
        compiler_params=pltpu.CompilerParams(vmem_limit_bytes=VMEM),
        name="lag_kernels",
    )(windows, lags, *earlier)


I_PIECE = NP * K
I_COUNT = 2 * NP * K
I_OWNER = I_COUNT + NP
I_SLOT = I_OWNER + NP
I_CORE = I_SLOT + SEG


def correlate_body(info_ref, kernel_ref, *refs):
    sources, keep_ref, send_ref = refs[:K], refs[K], refs[K + 1]
    o = pl.program_id(0)
    core = info_ref[I_CORE]
    total = 0.0
    for s in range(SEG):
        left = kernel_ref[0, s].reshape(LAGS * R_CH, KF)
        rows = []
        for q in range(SLOTS):
            for k in range(K):
                used = (k < info_ref[I_COUNT + o]) & (info_ref[I_SLOT + s] == q)
                rows.append(sources[k][0, 0, s].astype(F32) * used.astype(F32))
        right = jnp.concatenate(rows, axis=0).astype(BF)
        total = total + lax.dot_general(left, right, (((1,), (1,)), ((), ())), preferred_element_type=F32)
    total = total.reshape(NX, NC, R_CH, W)
    keep_ref[:, 0] = jnp.where(core == 0, total[:, 0], total[:, 1])
    send_ref[:, 0] = jnp.where(core == 0, total[:, 1], total[:, 0])


def correlate(info, kernels, gathered):
    def source_map(k):
        return lambda o, info: (info[o * K + k], info[I_PIECE + o * K + k], 0, 0, 0)

    out_spec = pl.BlockSpec((NX, 1, R_CH, W), lambda o, info: (0, info[I_OWNER + o], 0, 0))
    out = jax.ShapeDtypeStruct((NX, NP, R_CH, W), F32)
    return pl.pallas_call(
        correlate_body,
        grid_spec=pltpu.PrefetchScalarGridSpec(
            num_scalar_prefetch=1,
            grid=(NP,),
            in_specs=[pl.BlockSpec((1, SEG, LAGS, R_CH, KF), lambda o, info: (o, 0, 0, 0, 0))]
            + [pl.BlockSpec((1, 1, SEG, CQ, KF), source_map(k)) for k in range(K)],
            out_specs=[out_spec, out_spec],
        ),
        out_shape=[out, out],
        compiler_params=pltpu.CompilerParams(vmem_limit_bytes=VMEM),
        name="correlate",
    )(info, kernels, *([gathered] * K))


def finish_body(parts_ref, out_ref):
    pieces = [parts_ref[r].astype(F32) for r in range(NP)]
    for q in range(SLOTS):
        for k in range(K):
            at = (q * K + k) * CQ
            row = jnp.concatenate([v[:, at : at + CQ] for v in pieces], axis=1)
            out_ref[0, q, k] = row.astype(BF)


def finish(parts):
    return pl.pallas_call(
        finish_body,
        out_shape=jax.ShapeDtypeStruct((1, SLOTS, K, R_CH, CH), BF),
        compiler_params=pltpu.CompilerParams(vmem_limit_bytes=VMEM),
        name="finish",
    )(parts)


def around(size, distance):
    return [(i, (i + distance) % size) for i in range(size)]


def gather_planes(held):
    got = [held] + [None] * (NH - 1)
    ahead = behind = held
    for step in range(1, NH // 2):
        ahead = lax.ppermute(ahead, "zh", around(NH, 1))
        behind = lax.ppermute(behind, "zh", around(NH, -1))
        got[step], got[NH - step] = ahead, behind
    first = lax.ppermute(ahead[: NP // 2], "zh", around(NH, 1))
    second = lax.ppermute(behind[NP // 2 :], "zh", around(NH, -1))
    return got, first, second


def body(traces, source_list, source_count, receiver_start, segment_slot):
    y = lax.axis_index("y")
    zh = lax.axis_index("zh")
    zl = lax.axis_index("zl")
    t = lax.axis_index(("x", "c"))
    table = jnp.asarray(transform_table())
    lags = jnp.asarray(lag_tables())
    split, low, high = whiten(traces, table)
    pairs = NY * NZ
    following = lax.ppermute(low, ("y", "zh", "zl"), [(p, p - 1) for p in range(1, pairs)])
    crossed = lax.all_to_all(split, ("y", "zl"), 0, 0)

    joined = jnp.concatenate([high, following], axis=1)
    offset = lax.dynamic_index_in_dim(receiver_start, (y * NH + zh) * G + zl, keepdims=False) - CH // 2
    window = lax.dynamic_slice_in_dim(joined, offset, R_CH, 1)
    windows = jnp.stack([window] + [lax.ppermute(window, "zl", around(G, d)) for d in range(1, G)])
    crossed, windows = lax.optimization_barrier((crossed, windows))
    got, first, second = gather_planes(crossed)
    kernels = lag_kernels(0, windows, lags, None)
    for d in (1, 3, 2):
        kernels = lag_kernels(d, lax.ppermute(windows, "y", around(NY, d)), lags, kernels)

    kernels, first, second = lax.optimization_barrier((kernels, first, second))
    got[NH // 2] = jnp.concatenate([first, second], axis=0)
    gathered = jnp.stack(got)

    owner_y = jnp.repeat((y - jnp.arange(NY, dtype=jnp.int32)) % NY, G)
    owner_z = jnp.tile((zl - jnp.arange(G, dtype=jnp.int32)) % G, NY)
    owner = (owner_y * NH + zh) * G + owner_z
    lists = jnp.take(source_list, owner, axis=0).reshape(-1)
    counts = jnp.take(source_count, owner, axis=0)
    plane = lists % NZ
    place = (zh - plane // G) % NH
    piece = (lists // NZ) * G + plane % G
    slots = lax.dynamic_slice_in_dim(segment_slot, t * SEG, SEG, 0)
    core = lax.axis_index("c").astype(jnp.int32)[None]
    info = jnp.concatenate([place, piece, counts, owner_y * G + owner_z, slots, core]).astype(jnp.int32)
    keep, send = correlate(info, kernels, gathered)
    both = (keep + lax.ppermute(send, "c", around(NC, 1))).astype(BF)
    parts = lax.all_to_all(both, "x", 0, 0)
    total = jnp.sum(parts.astype(F32), axis=0).astype(BF)
    return finish(lax.all_to_all(total, ("y", "zl"), 0, 0))


def solution(mesh):
    grid = Mesh(mesh.devices.reshape(NY, NH, G, NX, NC), ("y", "zh", "zl", "x", "c"))
    tm, pair = ("x", "c"), ("y", "zh", "zl")
    return jax.shard_map(
        body,
        mesh=grid,
        in_specs=(P(tm, None, pair), P(), P(), P(), P()),
        out_specs=P(tm, None, pair, None, None),
        check_vma=False,
    )
```

```python
import jax
import jax.numpy as jnp
import numpy as np
from jax import lax
from jax.experimental import pallas as pl
from jax.experimental.pallas import tpu as pltpu
from jax.sharding import Mesh, PartitionSpec as P

CH = 128
SAMPLES = 2048
NF = 512
BAND = 32
K = 8
R_CH = 64
LAGS = 8
SLOTS = 2
F0 = 64
SEGS = 16
NY, NZ, NX, NC = 4, 16, 4, 2
SEG = 2
CQ = CH // NY
FB = 128
NB = NF // FB
KF = 2 * NF
EPS = 1e-06
NORM = np.float32((2.0 * NF * SEGS / SLOTS) ** (-0.5))
BF = jnp.bfloat16
F32 = jnp.float32
MIB = 1024 * 1024


def transform_table():
    bins = F0 + np.arange(NF, dtype=np.int64)
    phase = (bins[:, None] * np.arange(SAMPLES // 2, dtype=np.int64)[None, :]) % SAMPLES
    steps = np.arange(SAMPLES, dtype=np.float32) * np.float32(2.0 * np.pi / SAMPLES)
    cos = np.cos(steps)[phase]
    sin = -np.sin(steps)[phase]
    return np.stack([cos, sin], axis=0).astype(jnp.bfloat16)


def lag_tables():
    bins = F0 + np.arange(NF, dtype=np.int64)
    lags = np.arange(LAGS, dtype=np.int64) - LAGS // 2
    phase = (lags[:, None] * bins[None, :]) % SAMPLES
    angle = phase.astype(np.float32) * np.float32(2.0 * np.pi / SAMPLES)
    return np.stack([np.cos(angle), np.sin(angle)], axis=0).astype(np.float32)


def whiten_kernel(traces_ref, table_ref, split_ref, low_ref, high_ref):
    half = SAMPLES // 2
    table = table_ref[...].reshape(2 * FB, half)
    early = jnp.concatenate([traces_ref[s, :half] for s in range(SEG)], axis=1)
    late = jnp.concatenate([traces_ref[s, half:] for s in range(SEG)], axis=1)
    early = jnp.dot(table, early, preferred_element_type=F32)
    late = jnp.dot(table, late, preferred_element_type=F32)
    odd = lax.broadcasted_iota(jnp.int32, late.shape, 0) % 2 == 1
    spectra = early + jnp.where(odd, -late, late)
    grouped = spectra.reshape(2, FB // BAND, BAND, SEG * CH)
    power = jnp.sum(grouped * grouped, axis=(0, 2)) * (1.0 / (2 * BAND))
    scale = 1.0 / jnp.sqrt(power + EPS)
    whitened = grouped * scale[None, :, None, :]
    flipped = whitened.reshape(2 * FB, SEG * CH).T.astype(BF)
    for s in range(SEG):
        low_ref[s] = flipped[s * CH : s * CH + CH // 2]
        high_ref[s] = flipped[s * CH + CH // 2 : (s + 1) * CH]
        for y in range(NY):
            split_ref[y, s] = flipped[s * CH + y * CQ : s * CH + (y + 1) * CQ]


def whiten(traces, table):
    half = jax.ShapeDtypeStruct((SEG, CH // 2, KF), BF)
    half_spec = pl.BlockSpec((SEG, CH // 2, 2 * FB), lambda g: (0, 0, g))
    return pl.pallas_call(
        whiten_kernel,
        grid=(NB,),
        in_specs=[
            pl.BlockSpec((SEG, SAMPLES, CH), lambda g: (0, 0, 0)),
            pl.BlockSpec((2, FB, SAMPLES // 2), lambda g: (0, g, 0)),
        ],
        out_specs=[
            pl.BlockSpec((NY, SEG, CQ, 2 * FB), lambda g: (0, 0, 0, g)),
            half_spec,
            half_spec,
        ],
        out_shape=[jax.ShapeDtypeStruct((NY, SEG, CQ, KF), BF), half, half],
        compiler_params=pltpu.CompilerParams(vmem_limit_bytes=448 * MIB),
        name="whiten",
    )(traces, table)


def lag_kernel_body(window_ref, lag_ref, out_ref):
    for b in range(NB):
        at = b * 2 * FB
        real = window_ref[0, 0, :, at : at + FB].astype(F32)
        imag = window_ref[0, 0, :, at + FB : at + 2 * FB].astype(F32)
        for l in range(LAGS):
            cos = lag_ref[0, l : l + 1, b * FB : (b + 1) * FB]
            sin = lag_ref[1, l : l + 1, b * FB : (b + 1) * FB]
            for_real = (cos * real + sin * imag) * NORM
            for_imag = (cos * imag - sin * real) * NORM
            out_ref[0, 0, l, :, at : at + FB] = for_real.astype(BF)
            out_ref[0, 0, l, :, at + FB : at + 2 * FB] = for_imag.astype(BF)


def lag_kernels(windows, lags):
    return pl.pallas_call(
        lag_kernel_body,
        grid=(NY, SEG),
        in_specs=[
            pl.BlockSpec((1, 1, R_CH, KF), lambda o, s: (o, s, 0, 0)),
            pl.BlockSpec((2, LAGS, NF), lambda o, s: (0, 0, 0)),
        ],
        out_specs=pl.BlockSpec((1, 1, LAGS, R_CH, KF), lambda o, s: (o, s, 0, 0, 0)),
        out_shape=jax.ShapeDtypeStruct((NY, SEG, LAGS, R_CH, KF), BF),
        compiler_params=pltpu.CompilerParams(vmem_limit_bytes=48 * MIB),
        name="lag_kernels",
    )(windows, lags)


def correlate_body(info_ref, kernel_ref, *refs):
    sources, out_ref = refs[:K], refs[K]
    o = pl.program_id(0)
    lane = lax.broadcasted_iota(jnp.int32, (1, K * CQ), 1)
    live = (lane < info_ref[64 + o] * CQ).astype(F32)
    sums = []
    for s in range(SEG):
        left = kernel_ref[0, s, :, 0].reshape(NX * R_CH, KF)
        right = jnp.concatenate([ref[0, 0, s] for ref in sources], axis=0)
        sums.append(lax.dot_general(left, right, (((1,), (1,)), ((), ())), preferred_element_type=F32))
    for q in range(SLOTS):
        total = 0.0
        for s in range(SEG):
            total = total + sums[s] * (live * (info_ref[68 + s] == q).astype(F32))
        out_ref[0, :, q] = total.reshape(NX, R_CH, K * CQ)


def correlate(info, kernels, gathered, name):
    def source_map(k):
        return lambda o, info: (info[o * K + k], info[32 + o * K + k], 0, 0, 0)

    return pl.pallas_call(
        correlate_body,
        grid_spec=pltpu.PrefetchScalarGridSpec(
            num_scalar_prefetch=1,
            grid=(NY,),
            in_specs=[
                pl.BlockSpec(
                    (1, SEG, NX, 1, R_CH, KF),
                    lambda o, info: (lax.rem(info[70] + NY - o, NY), 0, 0, info[71], 0, 0),
                )
            ]
            + [pl.BlockSpec((1, 1, SEG, CQ, KF), source_map(k)) for k in range(K)],
            out_specs=pl.BlockSpec((1, NX, SLOTS, R_CH, K * CQ), lambda o, info: (o, 0, 0, 0, 0)),
        ),
        out_shape=jax.ShapeDtypeStruct((NY, NX, SLOTS, R_CH, K * CQ), F32),
        compiler_params=pltpu.CompilerParams(vmem_limit_bytes=448 * MIB),
        name=name,
    )(info, kernels, *([gathered] * K))


def finish_body(parts_ref, out_ref):
    quarter = []
    for y in range(NY):
        total = parts_ref[y * NX, 0].astype(F32)
        for x in range(1, NX):
            total = total + parts_ref[y * NX + x, 0].astype(F32)
        quarter.append(total)
    for k in range(K):
        row = jnp.concatenate([v[:, k * CQ : (k + 1) * CQ] for v in quarter], axis=1)
        out_ref[0, 0, k] = row.astype(BF)


def finish(parts):
    return pl.pallas_call(
        finish_body,
        grid=(SLOTS,),
        in_specs=[pl.BlockSpec((NY * NX, 1, R_CH, K * CQ), lambda q: (0, q, 0, 0))],
        out_specs=pl.BlockSpec((1, 1, K, R_CH, CH), lambda q: (0, q, 0, 0, 0)),
        out_shape=jax.ShapeDtypeStruct((1, SLOTS, K, R_CH, CH), BF),
        compiler_params=pltpu.CompilerParams(vmem_limit_bytes=48 * MIB),
        name="finish",
    )(parts)


def body(traces, source_list, source_count, receiver_start, segment_slot):
    y = lax.axis_index("y")
    z = lax.axis_index("z")
    t = lax.axis_index(("x", "c"))
    table = jnp.asarray(transform_table())
    lags = jnp.asarray(lag_tables())
    split, low, high = whiten(traces, table)
    crossed = lax.all_to_all(split, "y", 0, 0)
    gathered = lax.all_gather(crossed, "z", axis=0, tiled=False)

    low, high, _ = lax.optimization_barrier((low, high, crossed))
    pairs = NY * NZ
    following = lax.ppermute(low, ("y", "z"), [(p, p - 1) for p in range(1, pairs)])
    joined = jnp.concatenate([high, following], axis=1)
    offset = lax.dynamic_index_in_dim(receiver_start, y * NZ + z, keepdims=False) - CH // 2
    window = lax.dynamic_slice_in_dim(joined, offset, R_CH, 1)
    windows = jnp.stack(
        [window] + [lax.ppermute(window, "y", [(i, (i + d) % NY) for i in range(NY)]) for d in range(1, NY)]
    )
    kernels = lag_kernels(windows, lags)

    lists = lax.dynamic_index_in_dim(source_list.reshape(NY, NZ, K), z, 1, keepdims=False).reshape(-1)
    counts = lax.dynamic_index_in_dim(source_count.reshape(NY, NZ), z, 1, keepdims=False)
    slots = lax.dynamic_slice_in_dim(segment_slot, t * SEG, SEG, 0)
    core = lax.axis_index("c")[None].astype(jnp.int32)
    common = [lists % NZ, lists // NZ, counts, slots, y[None].astype(jnp.int32)]
    kernels = kernels.reshape(NY, SEG, NX, NC, R_CH, KF)
    send = correlate(jnp.concatenate(common + [1 - core]), kernels, gathered, "correlate_other")
    other = lax.ppermute(send, "c", [(0, 1), (1, 0)])
    keep = correlate(jnp.concatenate(common + [core]), kernels, gathered, "correlate_own")
    parts = (keep + other).astype(BF).reshape(NY * NX, SLOTS, R_CH, K * CQ)
    return finish(lax.all_to_all(parts, ("y", "x"), 0, 0))


def solution(mesh):
    grid = Mesh(mesh.devices.reshape(NY, NZ, NX, NC), ("y", "z", "x", "c"))
    tm, pair = ("x", "c"), ("y", "z")
    return jax.shard_map(
        body,
        mesh=grid,
        in_specs=(P(tm, None, pair), P(), P(), P(), P()),
        out_specs=P(tm, None, pair, None, None),
        check_vma=False,
    )
```

```python
import jax
import jax.numpy as jnp
import numpy as np
from jax import lax
from jax.experimental import pallas as pl
from jax.experimental.pallas import tpu as pltpu
from jax.sharding import Mesh, PartitionSpec as P

CH = 128
SAMPLES = 2048
NF = 512
BAND = 32
K = 8
R_CH = 64
LAGS = 8
SLOTS = 2
F0 = 64
SEGS = 16
NY, NZ, NX, NC = 4, 16, 4, 2
SEG = 2
SEG_CHIP = SEG * NC
PIECES = NY * NC
CQ = CH // PIECES
FB = 128
NB = NF // FB
KF = 2 * NF
EPS = 1e-06
NORM = np.float32((2.0 * NF * SEGS / SLOTS) ** (-0.5))
BF = jnp.bfloat16
F32 = jnp.float32
VMEM = 48 * 1024 * 1024


def transform_table():
    bins = F0 + np.arange(NF, dtype=np.int64)
    phase = (bins[:, None] * np.arange(SAMPLES // 2, dtype=np.int64)[None, :]) % SAMPLES
    steps = np.arange(SAMPLES, dtype=np.float32) * np.float32(2.0 * np.pi / SAMPLES)
    cos = np.cos(steps)[phase]
    sin = -np.sin(steps)[phase]
    return np.stack([cos, sin], axis=0).astype(jnp.bfloat16)


def lag_tables():
    bins = F0 + np.arange(NF, dtype=np.int64)
    lags = np.arange(LAGS, dtype=np.int64) - LAGS // 2
    phase = (lags[:, None] * bins[None, :]) % SAMPLES
    angle = phase.astype(np.float32) * np.float32(2.0 * np.pi / SAMPLES)
    return np.stack([np.cos(angle), np.sin(angle)], axis=0).astype(np.float32)


def whiten_kernel(traces_ref, table_ref, split_ref, low_ref, high_ref):
    half = SAMPLES // 2
    table = table_ref[...].reshape(2 * FB, half)
    early = jnp.concatenate([traces_ref[s, :half] for s in range(SEG)], axis=1)
    late = jnp.concatenate([traces_ref[s, half:] for s in range(SEG)], axis=1)
    early = jnp.dot(table, early, preferred_element_type=F32)
    late = jnp.dot(table, late, preferred_element_type=F32)
    odd = lax.broadcasted_iota(jnp.int32, late.shape, 0) % 2 == 1
    spectra = early + jnp.where(odd, -late, late)
    grouped = spectra.reshape(2, FB // BAND, BAND, SEG * CH)
    power = jnp.sum(grouped * grouped, axis=(0, 2)) * (1.0 / (2 * BAND))
    scale = 1.0 / jnp.sqrt(power + EPS)
    whitened = grouped * scale[None, :, None, :]
    flipped = whitened.reshape(2 * FB, SEG * CH).T.astype(BF)
    for s in range(SEG):
        low_ref[s] = flipped[s * CH : s * CH + CH // 2]
        high_ref[s] = flipped[s * CH + CH // 2 : (s + 1) * CH]
        for r in range(PIECES):
            split_ref[r, s] = flipped[s * CH + r * CQ : s * CH + (r + 1) * CQ]


def whiten(traces, table):
    half = jax.ShapeDtypeStruct((SEG, CH // 2, KF), BF)
    half_spec = pl.BlockSpec((SEG, CH // 2, 2 * FB), lambda g: (0, 0, g))
    return pl.pallas_call(
        whiten_kernel,
        grid=(NB,),
        in_specs=[
            pl.BlockSpec((SEG, SAMPLES, CH), lambda g: (0, 0, 0)),
            pl.BlockSpec((2, FB, SAMPLES // 2), lambda g: (0, g, 0)),
        ],
        out_specs=[
            pl.BlockSpec((PIECES, SEG, CQ, 2 * FB), lambda g: (0, 0, 0, g)),
            half_spec,
            half_spec,
        ],
        out_shape=[jax.ShapeDtypeStruct((PIECES, SEG, CQ, KF), BF), half, half],
        compiler_params=pltpu.CompilerParams(vmem_limit_bytes=VMEM),
        name="whiten",
    )(traces, table)


def lag_kernel_body(core_ref, window_ref, lag_ref, out_ref):
    for b in range(NB):
        at = b * 2 * FB
        real = window_ref[0, 0, :, at : at + FB].astype(F32)
        imag = window_ref[0, 0, :, at + FB : at + 2 * FB].astype(F32)
        for l in range(0, LAGS, 2):
            reals, imags = [], []
            for m in (l, l + 1):
                cos = lag_ref[0, m : m + 1, b * FB : (b + 1) * FB]
                sin = lag_ref[1, m : m + 1, b * FB : (b + 1) * FB]
                reals.append((cos * real + sin * imag) * NORM)
                imags.append((cos * imag - sin * real) * NORM)
            lanes = slice(l * R_CH, (l + 2) * R_CH)
            out_ref[0, 0, at : at + FB, lanes] = jnp.concatenate(reals, axis=0).T.astype(BF)
            out_ref[0, 0, at + FB : at + 2 * FB, lanes] = jnp.concatenate(imags, axis=0).T.astype(BF)


def lag_kernels(core, windows, lags):
    return pl.pallas_call(
        lag_kernel_body,
        grid_spec=pltpu.PrefetchScalarGridSpec(
            num_scalar_prefetch=1,
            grid=(NY, SEG_CHIP),
            in_specs=[
                pl.BlockSpec((1, 1, R_CH, KF), lambda o, s, core: (o, s, 0, 0)),
                pl.BlockSpec((2, LAGS, NF), lambda o, s, core: (0, 0, 0)),
            ],
            out_specs=pl.BlockSpec(
                (1, 1, KF, LAGS * R_CH),
                lambda o, s, core: (o, lax.rem(s + SEG * core[0], SEG_CHIP), 0, 0),
            ),
        ),
        out_shape=jax.ShapeDtypeStruct((NY, SEG_CHIP, KF, LAGS * R_CH), BF),
        compiler_params=pltpu.CompilerParams(vmem_limit_bytes=VMEM),
        name="lag_kernels",
    )(core, windows, lags)


I_COUNT = 2 * NY * K
I_SLOT = I_COUNT + NY
I_Y = I_SLOT + SEG_CHIP


def correlate_body(info_ref, kernel_ref, *refs):
    sources, out_ref = refs[:K], refs[K]
    o = pl.program_id(0)
    row = lax.broadcasted_iota(jnp.int32, (K * CQ, 1), 0)
    live = (row < info_ref[I_COUNT + o] * CQ).astype(F32)
    totals = [0.0] * SLOTS
    for s in range(SEG_CHIP):
        left = jnp.concatenate([ref[0, 0, s] for ref in sources], axis=0)
        part = jnp.dot(left, kernel_ref[0, s], preferred_element_type=F32)
        for q in range(SLOTS):
            totals[q] = totals[q] + part * (live * (info_ref[I_SLOT + s] == q).astype(F32))
    for l in range(LAGS):
        both = jnp.concatenate([v[:, l * R_CH : (l + 1) * R_CH] for v in totals], axis=1)
        out_ref[0, l] = both.astype(BF)


def correlate(info, kernels, gathered):
    def source_map(k):
        return lambda o, info: (info[o * K + k], info[NY * K + o * K + k], 0, 0, 0)

    return pl.pallas_call(
        correlate_body,
        grid_spec=pltpu.PrefetchScalarGridSpec(
            num_scalar_prefetch=1,
            grid=(NY,),
            in_specs=[
                pl.BlockSpec(
                    (1, SEG_CHIP, KF, LAGS * R_CH),
                    lambda o, info: (lax.rem(info[I_Y] + NY - o, NY), 0, 0, 0),
                )
            ]
            + [pl.BlockSpec((1, 1, SEG_CHIP, CQ, KF), source_map(k)) for k in range(K)],
            out_specs=pl.BlockSpec((1, LAGS, K * CQ, SLOTS * R_CH), lambda o, info: (o, 0, 0, 0)),
        ),
        out_shape=jax.ShapeDtypeStruct((NY, LAGS, K * CQ, SLOTS * R_CH), BF),
        compiler_params=pltpu.CompilerParams(vmem_limit_bytes=VMEM),
        name="correlate",
    )(info, kernels, *([gathered] * K))


def finish_body(parts_ref, out_ref):
    pieces = []
    for y in range(NY):
        for c in range(NC):
            total = parts_ref[y * NX * NC + c].astype(F32)
            for x in range(1, NX):
                total = total + parts_ref[(y * NX + x) * NC + c].astype(F32)
            pieces.append(total)
    for k in range(K):
        rows = jnp.concatenate([v[k * CQ : (k + 1) * CQ] for v in pieces], axis=0).T.astype(BF)
        for q in range(SLOTS):
            out_ref[0, q, k] = rows[q * R_CH : (q + 1) * R_CH]


def finish(parts):
    return pl.pallas_call(
        finish_body,
        out_shape=jax.ShapeDtypeStruct((1, SLOTS, K, R_CH, CH), BF),
        compiler_params=pltpu.CompilerParams(vmem_limit_bytes=VMEM),
        name="finish",
    )(parts)


def body(traces, source_list, source_count, receiver_start, segment_slot):
    y = lax.axis_index("y")
    z = lax.axis_index("z")
    table = jnp.asarray(transform_table())
    lags = jnp.asarray(lag_tables())
    split, low, high = whiten(traces, table)
    crossed = lax.all_to_all(split, ("y", "c"), 0, 0).reshape(NY, SEG_CHIP, CQ, KF)
    gathered = lax.all_gather(crossed, "z", axis=0, tiled=False)

    low, high, _ = lax.optimization_barrier((low, high, crossed))
    pairs = NY * NZ
    following = lax.ppermute(low, ("y", "z"), [(p, p - 1) for p in range(1, pairs)])
    joined = jnp.concatenate([high, following], axis=1)
    offset = lax.dynamic_index_in_dim(receiver_start, y * NZ + z, keepdims=False) - CH // 2
    window = lax.dynamic_slice_in_dim(joined, offset, R_CH, 1)
    own = jnp.stack(
        [window] + [lax.ppermute(window, "y", [(i, (i + d) % NY) for i in range(NY)]) for d in range(1, NY)]
    )
    other = lax.ppermute(own, "c", [(0, 1), (1, 0)])
    core = lax.axis_index("c")[None].astype(jnp.int32)
    kernels = lag_kernels(core, jnp.concatenate([own, other], axis=1), lags)

    lists = lax.dynamic_index_in_dim(source_list.reshape(NY, NZ, K), z, 1, keepdims=False).reshape(-1)
    counts = lax.dynamic_index_in_dim(source_count.reshape(NY, NZ), z, 1, keepdims=False)
    slots = lax.dynamic_slice_in_dim(segment_slot, lax.axis_index("x") * SEG_CHIP, SEG_CHIP, 0)
    info = jnp.concatenate([lists % NZ, lists // NZ, counts, slots, y[None].astype(jnp.int32)])
    sums = correlate(info, kernels, gathered)
    parts = lax.all_to_all(sums.reshape(NY * LAGS, K * CQ, SLOTS * R_CH), ("y", "x", "c"), 0, 0)
    return finish(parts)


def solution(mesh):
    grid = Mesh(mesh.devices.reshape(NY, NZ, NX, NC), ("y", "z", "x", "c"))
    tm, pair = ("x", "c"), ("y", "z")
    return jax.shard_map(
        body,
        mesh=grid,
        in_specs=(P(tm, None, pair), P(), P(), P(), P()),
        out_specs=P(tm, None, pair, None, None),
        check_vma=False,
    )
```

```python
import jax
import jax.numpy as jnp
import numpy as np
from jax import lax
from jax.experimental import pallas as pl
from jax.experimental.pallas import tpu as pltpu
from jax.sharding import Mesh, PartitionSpec as P

CH = 128
SAMPLES = 2048
NF = 512
BAND = 32
K = 8
R_CH = 64
LAGS = 8
SLOTS = 2
F0 = 64
SEGS = 16
NY, NZ, NX, NC = 4, 16, 4, 2
SEG = 2
SEG_CHIP = SEG * NC
PIECES = NY * NC
CQ = CH // PIECES
FB = 128
NB = NF // FB
KF = 2 * NF
EPS = 1e-06
NORM = np.float32((2.0 * NF * SEGS / SLOTS) ** (-0.5))
BF = jnp.bfloat16
F32 = jnp.float32
VMEM = 48 * 1024 * 1024


def transform_table():
    bins = F0 + np.arange(NF, dtype=np.int64)
    phase = (bins[:, None] * np.arange(SAMPLES // 2, dtype=np.int64)[None, :]) % SAMPLES
    steps = np.arange(SAMPLES, dtype=np.float32) * np.float32(2.0 * np.pi / SAMPLES)
    cos = np.cos(steps)[phase]
    sin = -np.sin(steps)[phase]
    return np.stack([cos, sin], axis=0).astype(jnp.bfloat16)


def lag_tables():
    bins = F0 + np.arange(NF, dtype=np.int64)
    lags = np.arange(LAGS, dtype=np.int64) - LAGS // 2
    phase = (lags[:, None] * bins[None, :]) % SAMPLES
    angle = phase.astype(np.float32) * np.float32(2.0 * np.pi / SAMPLES)
    return np.stack([np.cos(angle), np.sin(angle)], axis=0).astype(np.float32)


def whiten_kernel(traces_hbm, table_hbm, split_ref, low_ref, high_ref, traces_ref, table_ref, trace_sems, table_sems):
    half = SAMPLES // 2
    g = pl.program_id(0)

    def trace_copy(s, h):
        part = pl.ds(h * half, half)
        return pltpu.make_async_copy(traces_hbm.at[s, part], traces_ref.at[s, part], trace_sems.at[s, h])

    def table_copy(b):
        return pltpu.make_async_copy(table_hbm.at[:, pl.ds(b * FB, FB)], table_ref.at[b], table_sems.at[b])

    @pl.when(g == 0)
    def _():
        for s in range(SEG):
            for h in range(2):
                trace_copy(s, h).start()
        for b in range(NB):
            table_copy(b).start()
        for s in range(SEG):
            for h in range(2):
                trace_copy(s, h).wait()

    table_copy(g).wait()
    table = table_ref[g].reshape(2 * FB, half)
    early = jnp.concatenate([traces_ref[s, :half] for s in range(SEG)], axis=1)
    late = jnp.concatenate([traces_ref[s, half:] for s in range(SEG)], axis=1)
    early = jnp.dot(table, early, preferred_element_type=F32)
    late = jnp.dot(table, late, preferred_element_type=F32)
    odd = lax.broadcasted_iota(jnp.int32, late.shape, 0) % 2 == 1
    spectra = early + jnp.where(odd, -late, late)
    grouped = spectra.reshape(2, FB // BAND, BAND, SEG * CH)
    power = jnp.sum(grouped * grouped, axis=(0, 2)) * (1.0 / (2 * BAND))
    scale = 1.0 / jnp.sqrt(power + EPS)
    whitened = grouped * scale[None, :, None, :]
    flipped = whitened.reshape(2 * FB, SEG * CH).T.astype(BF)
    for s in range(SEG):
        low_ref[s] = flipped[s * CH : s * CH + CH // 2]
        high_ref[s] = flipped[s * CH + CH // 2 : (s + 1) * CH]
        for r in range(PIECES):
            split_ref[r, s] = flipped[s * CH + r * CQ : s * CH + (r + 1) * CQ]


def whiten(traces, table):
    half = jax.ShapeDtypeStruct((SEG, CH // 2, KF), BF)
    half_spec = pl.BlockSpec((SEG, CH // 2, 2 * FB), lambda g: (0, 0, g))
    return pl.pallas_call(
        whiten_kernel,
        grid=(NB,),
        in_specs=[pl.BlockSpec(memory_space=pl.ANY), pl.BlockSpec(memory_space=pl.ANY)],
        out_specs=[
            pl.BlockSpec((PIECES, SEG, CQ, 2 * FB), lambda g: (0, 0, 0, g)),
            half_spec,
            half_spec,
        ],
        out_shape=[jax.ShapeDtypeStruct((PIECES, SEG, CQ, KF), BF), half, half],
        scratch_shapes=[
            pltpu.VMEM((SEG, SAMPLES, CH), BF),
            pltpu.VMEM((NB, 2, FB, SAMPLES // 2), BF),
            pltpu.SemaphoreType.DMA((SEG, 2)),
            pltpu.SemaphoreType.DMA((NB,)),
        ],
        compiler_params=pltpu.CompilerParams(vmem_limit_bytes=VMEM),
        name="whiten",
    )(traces, table)


def lag_kernel_body(core_ref, window_ref, lag_ref, out_ref):
    for b in range(NB):
        at = b * 2 * FB
        real = window_ref[0, 0, :, at : at + FB].astype(F32)
        imag = window_ref[0, 0, :, at + FB : at + 2 * FB].astype(F32)
        for l in range(0, LAGS, 2):
            reals, imags = [], []
            for m in (l, l + 1):
                cos = lag_ref[0, m : m + 1, b * FB : (b + 1) * FB]
                sin = lag_ref[1, m : m + 1, b * FB : (b + 1) * FB]
                reals.append((cos * real + sin * imag) * NORM)
                imags.append((cos * imag - sin * real) * NORM)
            lanes = slice(l * R_CH, (l + 2) * R_CH)
            out_ref[0, 0, at : at + FB, lanes] = jnp.concatenate(reals, axis=0).T.astype(BF)
            out_ref[0, 0, at + FB : at + 2 * FB, lanes] = jnp.concatenate(imags, axis=0).T.astype(BF)


def lag_kernels(core, windows, lags):
    return pl.pallas_call(
        lag_kernel_body,
        grid_spec=pltpu.PrefetchScalarGridSpec(
            num_scalar_prefetch=1,
            grid=(NY, SEG_CHIP),
            in_specs=[
                pl.BlockSpec((1, 1, R_CH, KF), lambda o, s, core: (o, s, 0, 0)),
                pl.BlockSpec((2, LAGS, NF), lambda o, s, core: (0, 0, 0)),
            ],
            out_specs=pl.BlockSpec(
                (1, 1, KF, LAGS * R_CH),
                lambda o, s, core: (o, lax.rem(s + SEG * core[0], SEG_CHIP), 0, 0),
            ),
        ),
        out_shape=jax.ShapeDtypeStruct((NY, SEG_CHIP, KF, LAGS * R_CH), BF),
        compiler_params=pltpu.CompilerParams(vmem_limit_bytes=VMEM),
        name="lag_kernels",
    )(core, windows, lags)


I_COUNT = 2 * NY * K
I_SLOT = I_COUNT + NY
I_Y = I_SLOT + SEG_CHIP


def correlate_body(info_ref, kernel_ref, gathered_ref, out_ref, lagged_ref, source_ref, lag_sems, source_sems):
    o = pl.program_id(0)

    def source_copy(n):
        source = gathered_ref.at[info_ref[n], info_ref[NY * K + n]]
        return pltpu.make_async_copy(source, source_ref.at[n], source_sems.at[n])

    def lag_copy(n, s):
        owner = lax.rem(info_ref[I_Y] + NY - n, NY)
        return pltpu.make_async_copy(kernel_ref.at[owner, s], lagged_ref.at[n, s], lag_sems.at[n, s])

    @pl.when(o == 0)
    def _():
        for n in range(NY):
            for k in range(K):
                source_copy(n * K + k).start()
            for s in range(SEG_CHIP):
                lag_copy(n, s).start()

    for k in range(K):
        source_copy(o * K + k).wait()
    row = lax.broadcasted_iota(jnp.int32, (K * CQ, 1), 0)
    live = (row < info_ref[I_COUNT + o] * CQ).astype(F32)
    totals = [0.0] * SLOTS
    for s in range(SEG_CHIP):
        lag_copy(o, s).wait()
        left = jnp.concatenate([source_ref[o * K + k, s] for k in range(K)], axis=0)
        part = jnp.dot(left, lagged_ref[o, s], preferred_element_type=F32)
        for q in range(SLOTS):
            totals[q] = totals[q] + part * (live * (info_ref[I_SLOT + s] == q).astype(F32))
    for l in range(LAGS):
        both = jnp.concatenate([v[:, l * R_CH : (l + 1) * R_CH] for v in totals], axis=1)
        out_ref[0, l] = both.astype(BF)


def correlate(info, kernels, gathered):
    return pl.pallas_call(
        correlate_body,
        grid_spec=pltpu.PrefetchScalarGridSpec(
            num_scalar_prefetch=1,
            grid=(NY,),
            in_specs=[pl.BlockSpec(memory_space=pl.ANY), pl.BlockSpec(memory_space=pl.ANY)],
            out_specs=pl.BlockSpec((1, LAGS, K * CQ, SLOTS * R_CH), lambda o, info: (o, 0, 0, 0)),
            scratch_shapes=[
                pltpu.VMEM((NY, SEG_CHIP, KF, LAGS * R_CH), BF),
                pltpu.VMEM((NY * K, SEG_CHIP, CQ, KF), BF),
                pltpu.SemaphoreType.DMA((NY, SEG_CHIP)),
                pltpu.SemaphoreType.DMA((NY * K,)),
            ],
        ),
        out_shape=jax.ShapeDtypeStruct((NY, LAGS, K * CQ, SLOTS * R_CH), BF),
        compiler_params=pltpu.CompilerParams(vmem_limit_bytes=VMEM),
        name="correlate",
    )(info, kernels, gathered)


def finish_body(parts_ref, out_ref):
    pieces = []
    for y in range(NY):
        for c in range(NC):
            total = parts_ref[y * NX * NC + c].astype(F32)
            for x in range(1, NX):
                total = total + parts_ref[(y * NX + x) * NC + c].astype(F32)
            pieces.append(total)
    for k in range(K):
        rows = jnp.concatenate([v[k * CQ : (k + 1) * CQ] for v in pieces], axis=0).T.astype(BF)
        for q in range(SLOTS):
            out_ref[0, q, k] = rows[q * R_CH : (q + 1) * R_CH]


def finish(parts):
    return pl.pallas_call(
        finish_body,
        out_shape=jax.ShapeDtypeStruct((1, SLOTS, K, R_CH, CH), BF),
        compiler_params=pltpu.CompilerParams(vmem_limit_bytes=VMEM),
        name="finish",
    )(parts)


def body(traces, source_list, source_count, receiver_start, segment_slot):
    y = lax.axis_index("y")
    z = lax.axis_index("z")
    table = jnp.asarray(transform_table())
    lags = jnp.asarray(lag_tables())
    split, low, high = whiten(traces, table)
    crossed = lax.all_to_all(split, ("y", "c"), 0, 0).reshape(NY, SEG_CHIP, CQ, KF)
    gathered = lax.all_gather(crossed, "z", axis=0, tiled=False)

    low, high, _ = lax.optimization_barrier((low, high, crossed))
    pairs = NY * NZ
    following = lax.ppermute(low, ("y", "z"), [(p, p - 1) for p in range(1, pairs)])
    joined = jnp.concatenate([high, following], axis=1)
    offset = lax.dynamic_index_in_dim(receiver_start, y * NZ + z, keepdims=False) - CH // 2
    window = lax.dynamic_slice_in_dim(joined, offset, R_CH, 1)
    own = jnp.stack(
        [window] + [lax.ppermute(window, "y", [(i, (i + d) % NY) for i in range(NY)]) for d in range(1, NY)]
    )
    other = lax.ppermute(own, "c", [(0, 1), (1, 0)])
    core = lax.axis_index("c")[None].astype(jnp.int32)
    kernels = lag_kernels(core, jnp.concatenate([own, other], axis=1), lags)

    lists = lax.dynamic_index_in_dim(source_list.reshape(NY, NZ, K), z, 1, keepdims=False).reshape(-1)
    counts = lax.dynamic_index_in_dim(source_count.reshape(NY, NZ), z, 1, keepdims=False)
    slots = lax.dynamic_slice_in_dim(segment_slot, lax.axis_index("x") * SEG_CHIP, SEG_CHIP, 0)
    info = jnp.concatenate([lists % NZ, lists // NZ, counts, slots, y[None].astype(jnp.int32)])
    sums = correlate(info, kernels, gathered)
    parts = lax.all_to_all(sums.reshape(NY * LAGS, K * CQ, SLOTS * R_CH), ("y", "x", "c"), 0, 0)
    return finish(parts)


def solution(mesh):
    grid = Mesh(mesh.devices.reshape(NY, NZ, NX, NC), ("y", "z", "x", "c"))
    tm, pair = ("x", "c"), ("y", "z")
    return jax.shard_map(
        body,
        mesh=grid,
        in_specs=(P(tm, None, pair), P(), P(), P(), P()),
        out_specs=P(tm, None, pair, None, None),
        check_vma=False,
    )
```

```python
import jax
import jax.numpy as jnp
import numpy as np
from jax import lax
from jax.experimental import pallas as pl
from jax.experimental.pallas import tpu as pltpu
from jax.sharding import Mesh, PartitionSpec as P

CH = 128
SAMPLES = 2048
NF = 512
BAND = 32
K = 8
R_CH = 64
LAGS = 8
SLOTS = 2
F0 = 64
SEGS = 16
NY, NZ, NX, NC = 4, 16, 4, 2
SEG = 2
SEG_CHIP = SEG * NC
MOST = 3
SCALE = 4096.0
PIECES = NY * NC
CQ = CH // PIECES
FB = 128
NB = NF // FB
KF = 2 * NF
EPS = 1e-06
NORM = np.float32((2.0 * NF * SEGS / SLOTS) ** (-0.5))
BF = jnp.bfloat16
F32 = jnp.float32
VMEM = 48 * 1024 * 1024


def transform_table():
    bins = F0 + np.arange(NF, dtype=np.int64)
    phase = (bins[:, None] * np.arange(SAMPLES // 2, dtype=np.int64)[None, :]) % SAMPLES
    steps = np.arange(SAMPLES, dtype=np.float32) * np.float32(2.0 * np.pi / SAMPLES)
    cos = np.cos(steps)[phase]
    sin = -np.sin(steps)[phase]
    return np.stack([cos, sin], axis=0).astype(jnp.bfloat16)


def lag_tables():
    bins = F0 + np.arange(NF, dtype=np.int64)
    lags = np.arange(LAGS, dtype=np.int64) - LAGS // 2
    phase = (lags[:, None] * bins[None, :]) % SAMPLES
    angle = phase.astype(np.float32) * np.float32(2.0 * np.pi / SAMPLES)
    return (np.stack([np.cos(angle), np.sin(angle)], axis=0) * NORM).astype(np.float32)


def whiten_kernel(traces_hbm, table_hbm, split_ref, low_ref, high_ref, traces_ref, table_ref, trace_sems, table_sems):
    half = SAMPLES // 2
    g = pl.program_id(0)

    def trace_copy(s, h):
        part = pl.ds(h * half, half)
        return pltpu.make_async_copy(traces_hbm.at[s, part], traces_ref.at[s, part], trace_sems.at[s, h])

    def table_copy(b):
        return pltpu.make_async_copy(table_hbm.at[:, pl.ds(b * FB, FB)], table_ref.at[b], table_sems.at[b])

    @pl.when(g == 0)
    def _():
        for s in range(SEG):
            for h in range(2):
                trace_copy(s, h).start()
        for b in range(NB):
            table_copy(b).start()
        for s in range(SEG):
            for h in range(2):
                trace_copy(s, h).wait()

    table_copy(g).wait()
    table = table_ref[g].reshape(2 * FB, half)
    early = jnp.concatenate([traces_ref[s, :half] for s in range(SEG)], axis=1)
    late = jnp.concatenate([traces_ref[s, half:] for s in range(SEG)], axis=1)
    early = jnp.dot(table, early, preferred_element_type=F32)
    late = jnp.dot(table, late, preferred_element_type=F32)
    odd = lax.broadcasted_iota(jnp.int32, late.shape, 0) % 2 == 1
    spectra = early + jnp.where(odd, -late, late)
    grouped = spectra.reshape(2, FB // BAND, BAND, SEG * CH)
    power = jnp.sum(grouped * grouped, axis=(0, 2)) * (1.0 / (2 * BAND))
    scale = 1.0 / jnp.sqrt(power + EPS)
    whitened = grouped * scale[None, :, None, :]
    flipped = whitened.reshape(2 * FB, SEG * CH).T.astype(BF)
    for s in range(SEG):
        low_ref[s] = flipped[s * CH : s * CH + CH // 2]
        high_ref[s] = flipped[s * CH + CH // 2 : (s + 1) * CH]
        for r in range(PIECES):
            split_ref[r, s] = flipped[s * CH + r * CQ : s * CH + (r + 1) * CQ]


def whiten(traces, table):
    half = jax.ShapeDtypeStruct((SEG, CH // 2, KF), BF)
    half_spec = pl.BlockSpec((SEG, CH // 2, 2 * FB), lambda g: (0, 0, g))
    return pl.pallas_call(
        whiten_kernel,
        grid=(NB,),
        in_specs=[pl.BlockSpec(memory_space=pl.ANY), pl.BlockSpec(memory_space=pl.ANY)],
        out_specs=[
            pl.BlockSpec((PIECES, SEG, CQ, 2 * FB), lambda g: (0, 0, 0, g)),
            half_spec,
            half_spec,
        ],
        out_shape=[jax.ShapeDtypeStruct((PIECES, SEG, CQ, KF), BF), half, half],
        scratch_shapes=[
            pltpu.VMEM((SEG, SAMPLES, CH), BF),
            pltpu.VMEM((NB, 2, FB, SAMPLES // 2), BF),
            pltpu.SemaphoreType.DMA((SEG, 2)),
            pltpu.SemaphoreType.DMA((NB,)),
        ],
        compiler_params=pltpu.CompilerParams(vmem_limit_bytes=VMEM),
        name="whiten",
    )(traces, table)


def lag_kernel_body(core_ref, window_ref, lag_ref, out_ref, wide_ref):
    @pl.when((pl.program_id(0) == 0) & (pl.program_id(1) == 0))
    def _():
        for part in range(2):
            columns = lag_ref[part].T
            for l in range(0, LAGS, 2):
                both = [jnp.broadcast_to(columns[:, m : m + 1], (NF, R_CH)) for m in (l, l + 1)]
                wide_ref[part, :, l * R_CH : (l + 2) * R_CH] = jnp.concatenate(both, axis=1)

    for b in range(NB):
        at = b * 2 * FB
        bins = slice(b * FB, (b + 1) * FB)
        window = window_ref[0, 0, :, at : at + 2 * FB].astype(F32).T
        window = jnp.concatenate([window, window], axis=1)
        real, imag = window[:FB], window[FB:]
        for l in range(0, LAGS, 2):
            lanes = slice(l * R_CH, (l + 2) * R_CH)
            cos, sin = wide_ref[0, bins, lanes], wide_ref[1, bins, lanes]
            out_ref[0, 0, at : at + FB, lanes] = (cos * real + sin * imag).astype(BF)
            out_ref[0, 0, at + FB : at + 2 * FB, lanes] = (cos * imag - sin * real).astype(BF)


def lag_kernels(core, windows, lags):
    return pl.pallas_call(
        lag_kernel_body,
        grid_spec=pltpu.PrefetchScalarGridSpec(
            num_scalar_prefetch=1,
            grid=(NY, SEG_CHIP),
            in_specs=[
                pl.BlockSpec((1, 1, R_CH, KF), lambda o, s, core: (o, s, 0, 0)),
                pl.BlockSpec((2, LAGS, NF), lambda o, s, core: (0, 0, 0)),
            ],
            out_specs=pl.BlockSpec(
                (1, 1, KF, LAGS * R_CH),
                lambda o, s, core: (o, lax.rem(s + SEG * core[0], SEG_CHIP), 0, 0),
            ),
            scratch_shapes=[pltpu.VMEM((2, NF, LAGS * R_CH), F32)],
        ),
        out_shape=jax.ShapeDtypeStruct((NY, SEG_CHIP, KF, LAGS * R_CH), BF),
        compiler_params=pltpu.CompilerParams(vmem_limit_bytes=VMEM),
        name="lag_kernels",
    )(core, windows, lags)


I_COUNT = 2 * NY * K
I_SLOT = I_COUNT + NY
I_Y = I_SLOT + SEG_CHIP


def correlate_body(info_ref, kernel_ref, most_ref, last_ref, out_ref, lagged_ref, source_ref, lag_sems, source_sems):
    o = pl.program_id(0)

    def source_copies(n):
        most = most_ref.at[info_ref[n], info_ref[NY * K + n]]
        last = last_ref.at[info_ref[n], info_ref[NY * K + n]]
        into = source_ref.at[n]
        return (
            pltpu.make_async_copy(most, into.at[pl.ds(0, MOST)], source_sems.at[0, n]),
            pltpu.make_async_copy(last, into.at[pl.ds(MOST, SEG_CHIP - MOST)], source_sems.at[1, n]),
        )

    def lag_copy(n, s):
        owner = lax.rem(info_ref[I_Y] + NY - n, NY)
        return pltpu.make_async_copy(kernel_ref.at[owner, s], lagged_ref.at[n, s], lag_sems.at[n, s])

    @pl.when(o == 0)
    def _():
        for n in range(NY):
            for k in range(K):
                for copy in source_copies(n * K + k):
                    copy.start()
            for s in range(SEG_CHIP):
                lag_copy(n, s).start()

    for k in range(K):
        for copy in source_copies(o * K + k):
            copy.wait()
    row = lax.broadcasted_iota(jnp.int32, (K * CQ, 1), 0)
    live = (row < info_ref[I_COUNT + o] * CQ).astype(F32)
    totals = [0.0] * SLOTS
    for s in range(SEG_CHIP):
        lag_copy(o, s).wait()
        left = jnp.concatenate([source_ref[o * K + k, s] for k in range(K)], axis=0)
        part = jnp.dot(left, lagged_ref[o, s], preferred_element_type=F32)
        for q in range(SLOTS):
            totals[q] = totals[q] + part * (live * (info_ref[I_SLOT + s] == q).astype(F32))
    for l in range(LAGS):
        both = jnp.concatenate([v[:, l * R_CH : (l + 1) * R_CH] for v in totals], axis=1)
        out_ref[0, l] = both.astype(BF)


def correlate(info, kernels, most, last):
    return pl.pallas_call(
        correlate_body,
        grid_spec=pltpu.PrefetchScalarGridSpec(
            num_scalar_prefetch=1,
            grid=(NY,),
            in_specs=[pl.BlockSpec(memory_space=pl.ANY)] * 3,
            out_specs=pl.BlockSpec((1, LAGS, K * CQ, SLOTS * R_CH), lambda o, info: (o, 0, 0, 0)),
            scratch_shapes=[
                pltpu.VMEM((NY, SEG_CHIP, KF, LAGS * R_CH), BF),
                pltpu.VMEM((NY * K, SEG_CHIP, CQ, KF), BF),
                pltpu.SemaphoreType.DMA((NY, SEG_CHIP)),
                pltpu.SemaphoreType.DMA((2, NY * K)),
            ],
        ),
        out_shape=jax.ShapeDtypeStruct((NY, LAGS, K * CQ, SLOTS * R_CH), BF),
        compiler_params=pltpu.CompilerParams(vmem_limit_bytes=VMEM),
        name="correlate",
    )(info, kernels, most, last)


def finish_body(parts_ref, out_ref):
    pieces = []
    for y in range(NY):
        for c in range(NC):
            total = parts_ref[y * NX * NC + c].astype(F32)
            for x in range(1, NX):
                total = total + parts_ref[(y * NX + x) * NC + c].astype(F32)
            pieces.append(total)
    for k in range(K):
        rows = jnp.concatenate([v[k * CQ : (k + 1) * CQ] for v in pieces], axis=0).T.astype(BF)
        for q in range(SLOTS):
            out_ref[0, q, k] = rows[q * R_CH : (q + 1) * R_CH]


def finish(parts):
    return pl.pallas_call(
        finish_body,
        out_shape=jax.ShapeDtypeStruct((1, SLOTS, K, R_CH, CH), BF),
        compiler_params=pltpu.CompilerParams(vmem_limit_bytes=VMEM),
        name="finish",
    )(parts)


def body(traces, source_list, source_count, receiver_start, segment_slot):
    y = lax.axis_index("y")
    z = lax.axis_index("z")
    table = jnp.asarray(transform_table())
    lags = jnp.asarray(lag_tables())
    split, low, high = whiten(traces, table)
    crossed = lax.all_to_all(split, ("y", "c"), 0, 0).reshape(NY, SEG_CHIP, CQ, KF)
    most = lax.all_gather(crossed[:, :MOST], "z", axis=0, tiled=False)
    last = (crossed[:, MOST:] * jnp.bfloat16(SCALE)).astype(jnp.float16)
    last = lax.all_gather(last, "z", axis=0, tiled=False)

    low, high, _ = lax.optimization_barrier((low, high, crossed))
    pairs = NY * NZ
    following = lax.ppermute(low, ("y", "z"), [(p, p - 1) for p in range(1, pairs)])
    following, last = lax.optimization_barrier((following, last))
    last = (last.astype(F32) * (1.0 / SCALE)).astype(BF)
    joined = jnp.concatenate([high, following], axis=1)
    offset = lax.dynamic_index_in_dim(receiver_start, y * NZ + z, keepdims=False) - CH // 2
    window = lax.dynamic_slice_in_dim(joined, offset, R_CH, 1)
    own = jnp.stack(
        [window] + [lax.ppermute(window, "y", [(i, (i + d) % NY) for i in range(NY)]) for d in range(1, NY)]
    )
    other = lax.ppermute(own, "c", [(0, 1), (1, 0)])
    core = lax.axis_index("c")[None].astype(jnp.int32)
    kernels = lag_kernels(core, jnp.concatenate([own, other], axis=1), lags)

    lists = lax.dynamic_index_in_dim(source_list.reshape(NY, NZ, K), z, 1, keepdims=False).reshape(-1)
    counts = lax.dynamic_index_in_dim(source_count.reshape(NY, NZ), z, 1, keepdims=False)
    slots = lax.dynamic_slice_in_dim(segment_slot, lax.axis_index("x") * SEG_CHIP, SEG_CHIP, 0)
    info = jnp.concatenate([lists % NZ, lists // NZ, counts, slots, y[None].astype(jnp.int32)])
    sums = correlate(info, kernels, most, last)
    parts = lax.all_to_all(sums.reshape(NY * LAGS, K * CQ, SLOTS * R_CH), ("y", "x", "c"), 0, 0)
    return finish(parts)


def solution(mesh):
    grid = Mesh(mesh.devices.reshape(NY, NZ, NX, NC), ("y", "z", "x", "c"))
    tm, pair = ("x", "c"), ("y", "z")
    return jax.shard_map(
        body,
        mesh=grid,
        in_specs=(P(tm, None, pair), P(), P(), P(), P()),
        out_specs=P(tm, None, pair, None, None),
        check_vma=False,
    )
```

```python
import jax
import jax.numpy as jnp
import numpy as np
from jax import lax
from jax.experimental import pallas as pl
from jax.experimental.pallas import tpu as pltpu
from jax.sharding import Mesh, PartitionSpec as P

CH = 128
SAMPLES = 2048
NF = 512
BAND = 32
K = 8
R_CH = 64
LAGS = 8
SLOTS = 2
F0 = 64
SEGS = 16
NY, NZ, NX, NC = 4, 16, 4, 2
SEG = 2
SEG_CHIP = SEG * NC
PIECES = NY * NC
CQ = CH // PIECES
FB = 128
NB = NF // FB
KF = 2 * NF
EPS = 1e-06
NORM = np.float32((2.0 * NF * SEGS / SLOTS) ** (-0.5))
BF = jnp.bfloat16
F32 = jnp.float32
VMEM = 48 * 1024 * 1024


def transform_table():
    bins = F0 + np.arange(NF, dtype=np.int64)
    phase = (bins[:, None] * np.arange(SAMPLES // 2, dtype=np.int64)[None, :]) % SAMPLES
    steps = np.arange(SAMPLES, dtype=np.float32) * np.float32(2.0 * np.pi / SAMPLES)
    cos = np.cos(steps)[phase]
    sin = -np.sin(steps)[phase]
    return np.stack([cos, sin], axis=0).astype(jnp.bfloat16)


def lag_tables():
    bins = F0 + np.arange(NF, dtype=np.int64)
    lags = np.arange(LAGS, dtype=np.int64) - LAGS // 2
    phase = (lags[:, None] * bins[None, :]) % SAMPLES
    angle = phase.astype(np.float32) * np.float32(2.0 * np.pi / SAMPLES)
    return np.stack([np.cos(angle), np.sin(angle)], axis=0).astype(np.float32)


def whiten_kernel(traces_hbm, table_hbm, split_ref, low_ref, high_ref, traces_ref, table_ref, trace_sems, table_sems):
    half = SAMPLES // 2
    g = pl.program_id(0)

    def trace_copy(s, h):
        part = pl.ds(h * half, half)
        return pltpu.make_async_copy(traces_hbm.at[s, part], traces_ref.at[s, part], trace_sems.at[s, h])

    def table_copy(b):
        return pltpu.make_async_copy(table_hbm.at[:, pl.ds(b * FB, FB)], table_ref.at[b], table_sems.at[b])

    @pl.when(g == 0)
    def _():
        for s in range(SEG):
            for h in range(2):
                trace_copy(s, h).start()
        for b in range(NB):
            table_copy(b).start()
        for s in range(SEG):
            for h in range(2):
                trace_copy(s, h).wait()

    table_copy(g).wait()
    table = table_ref[g].reshape(2 * FB, half)
    early = jnp.concatenate([traces_ref[s, :half] for s in range(SEG)], axis=1)
    late = jnp.concatenate([traces_ref[s, half:] for s in range(SEG)], axis=1)
    early = jnp.dot(table, early, preferred_element_type=F32)
    late = jnp.dot(table, late, preferred_element_type=F32)
    odd = lax.broadcasted_iota(jnp.int32, late.shape, 0) % 2 == 1
    spectra = early + jnp.where(odd, -late, late)
    grouped = spectra.reshape(2, FB // BAND, BAND, SEG * CH)
    power = jnp.sum(grouped * grouped, axis=(0, 2)) * (1.0 / (2 * BAND))
    scale = 1.0 / jnp.sqrt(power + EPS)
    whitened = grouped * scale[None, :, None, :]
    flipped = whitened.reshape(2 * FB, SEG * CH).T.astype(BF)
    for s in range(SEG):
        low_ref[s] = flipped[s * CH : s * CH + CH // 2]
        high_ref[s] = flipped[s * CH + CH // 2 : (s + 1) * CH]
        for r in range(PIECES):
            split_ref[r, s] = flipped[s * CH + r * CQ : s * CH + (r + 1) * CQ]


def whiten(traces, table):
    half = jax.ShapeDtypeStruct((SEG, CH // 2, KF), BF)
    half_spec = pl.BlockSpec((SEG, CH // 2, 2 * FB), lambda g: (0, 0, g))
    return pl.pallas_call(
        whiten_kernel,
        grid=(NB,),
        in_specs=[pl.BlockSpec(memory_space=pl.ANY), pl.BlockSpec(memory_space=pl.ANY)],
        out_specs=[
            pl.BlockSpec((PIECES, SEG, CQ, 2 * FB), lambda g: (0, 0, 0, g)),
            half_spec,
            half_spec,
        ],
        out_shape=[jax.ShapeDtypeStruct((PIECES, SEG, CQ, KF), BF), half, half],
        scratch_shapes=[
            pltpu.VMEM((SEG, SAMPLES, CH), BF),
            pltpu.VMEM((NB, 2, FB, SAMPLES // 2), BF),
            pltpu.SemaphoreType.DMA((SEG, 2)),
            pltpu.SemaphoreType.DMA((NB,)),
        ],
        compiler_params=pltpu.CompilerParams(vmem_limit_bytes=61 * 1024 * 1024),
        name="whiten",
    )(traces, table)


def lag_kernel_body(core_ref, window_ref, lag_ref, out_ref):
    for b in range(NB):
        at = b * 2 * FB
        real = window_ref[0, 0, :, at : at + FB].astype(F32)
        imag = window_ref[0, 0, :, at + FB : at + 2 * FB].astype(F32)
        for l in range(0, LAGS, 2):
            reals, imags = [], []
            for m in (l, l + 1):
                cos = lag_ref[0, m : m + 1, b * FB : (b + 1) * FB]
                sin = lag_ref[1, m : m + 1, b * FB : (b + 1) * FB]
                reals.append((cos * real + sin * imag) * NORM)
                imags.append((cos * imag - sin * real) * NORM)
            lanes = slice(l * R_CH, (l + 2) * R_CH)
            out_ref[0, 0, at : at + FB, lanes] = jnp.concatenate(reals, axis=0).T.astype(BF)
            out_ref[0, 0, at + FB : at + 2 * FB, lanes] = jnp.concatenate(imags, axis=0).T.astype(BF)


def lag_kernels(core, windows, lags):
    return pl.pallas_call(
        lag_kernel_body,
        grid_spec=pltpu.PrefetchScalarGridSpec(
            num_scalar_prefetch=1,
            grid=(NY, SEG_CHIP),
            in_specs=[
                pl.BlockSpec((1, 1, R_CH, KF), lambda o, s, core: (o, s, 0, 0)),
                pl.BlockSpec((2, LAGS, NF), lambda o, s, core: (0, 0, 0)),
            ],
            out_specs=pl.BlockSpec(
                (1, 1, KF, LAGS * R_CH),
                lambda o, s, core: (o, lax.rem(s + SEG * core[0], SEG_CHIP), 0, 0),
            ),
        ),
        out_shape=jax.ShapeDtypeStruct((NY, SEG_CHIP, KF, LAGS * R_CH), BF),
        compiler_params=pltpu.CompilerParams(vmem_limit_bytes=VMEM),
        name="lag_kernels",
    )(core, windows, lags)


I_COUNT = 2 * NY * K
I_SLOT = I_COUNT + NY
I_Y = I_SLOT + SEG_CHIP


def correlate_body(info_ref, kernel_ref, *refs):
    sources, out_ref = refs[:K], refs[K]
    o = pl.program_id(0)
    row = lax.broadcasted_iota(jnp.int32, (K * CQ, 1), 0)
    live = (row < info_ref[I_COUNT + o] * CQ).astype(F32)
    totals = [0.0] * SLOTS
    for s in range(SEG_CHIP):
        left = jnp.concatenate([ref[0, 0, s] for ref in sources], axis=0)
        part = jnp.dot(left, kernel_ref[0, s], preferred_element_type=F32)
        for q in range(SLOTS):
            totals[q] = totals[q] + part * (live * (info_ref[I_SLOT + s] == q).astype(F32))
    for l in range(LAGS):
        both = jnp.concatenate([v[:, l * R_CH : (l + 1) * R_CH] for v in totals], axis=1)
        out_ref[0, l] = both.astype(BF)


def correlate(info, kernels, gathered):
    def source_map(k):
        return lambda o, info: (info[o * K + k], info[NY * K + o * K + k], 0, 0, 0)

    return pl.pallas_call(
        correlate_body,
        grid_spec=pltpu.PrefetchScalarGridSpec(
            num_scalar_prefetch=1,
            grid=(NY,),
            in_specs=[
                pl.BlockSpec(
                    (1, SEG_CHIP, KF, LAGS * R_CH),
                    lambda o, info: (lax.rem(info[I_Y] + NY - o, NY), 0, 0, 0),
                )
            ]
            + [pl.BlockSpec((1, 1, SEG_CHIP, CQ, KF), source_map(k)) for k in range(K)],
            out_specs=pl.BlockSpec((1, LAGS, K * CQ, SLOTS * R_CH), lambda o, info: (o, 0, 0, 0)),
        ),
        out_shape=jax.ShapeDtypeStruct((NY, LAGS, K * CQ, SLOTS * R_CH), BF),
        compiler_params=pltpu.CompilerParams(vmem_limit_bytes=VMEM),
        name="correlate",
    )(info, kernels, *([gathered] * K))


def finish_body(parts_ref, out_ref):
    pieces = []
    for y in range(NY):
        for c in range(NC):
            total = parts_ref[y * NX * NC + c].astype(F32)
            for x in range(1, NX):
                total = total + parts_ref[(y * NX + x) * NC + c].astype(F32)
            pieces.append(total)
    for k in range(K):
        rows = jnp.concatenate([v[k * CQ : (k + 1) * CQ] for v in pieces], axis=0).T.astype(BF)
        for q in range(SLOTS):
            out_ref[0, q, k] = rows[q * R_CH : (q + 1) * R_CH]


def finish(parts):
    return pl.pallas_call(
        finish_body,
        out_shape=jax.ShapeDtypeStruct((1, SLOTS, K, R_CH, CH), BF),
        compiler_params=pltpu.CompilerParams(vmem_limit_bytes=VMEM),
        name="finish",
    )(parts)


def body(traces, source_list, source_count, receiver_start, segment_slot):
    y = lax.axis_index("y")
    z = lax.axis_index("z")
    table = jnp.asarray(transform_table())
    lags = jnp.asarray(lag_tables())
    split, low, high = whiten(traces, table)
    crossed = lax.all_to_all(split, ("y", "c"), 0, 0).reshape(NY, SEG_CHIP, CQ, KF)
    gathered = lax.all_gather(crossed, "z", axis=0, tiled=False)

    low, high, _ = lax.optimization_barrier((low, high, crossed))
    pairs = NY * NZ
    following = lax.ppermute(low, ("y", "z"), [(p, p - 1) for p in range(1, pairs)])
    joined = jnp.concatenate([high, following], axis=1)
    offset = lax.dynamic_index_in_dim(receiver_start, y * NZ + z, keepdims=False) - CH // 2
    window = lax.dynamic_slice_in_dim(joined, offset, R_CH, 1)
    own = jnp.stack(
        [window] + [lax.ppermute(window, "y", [(i, (i + d) % NY) for i in range(NY)]) for d in range(1, NY)]
    )
    other = lax.ppermute(own, "c", [(0, 1), (1, 0)])
    core = lax.axis_index("c")[None].astype(jnp.int32)
    kernels = lag_kernels(core, jnp.concatenate([own, other], axis=1), lags)

    lists = lax.dynamic_index_in_dim(source_list.reshape(NY, NZ, K), z, 1, keepdims=False).reshape(-1)
    counts = lax.dynamic_index_in_dim(source_count.reshape(NY, NZ), z, 1, keepdims=False)
    slots = lax.dynamic_slice_in_dim(segment_slot, lax.axis_index("x") * SEG_CHIP, SEG_CHIP, 0)
    info = jnp.concatenate([lists % NZ, lists // NZ, counts, slots, y[None].astype(jnp.int32)])
    sums = correlate(info, kernels, gathered)
    parts = lax.all_to_all(sums.reshape(NY * LAGS, K * CQ, SLOTS * R_CH), ("y", "x", "c"), 0, 0)
    return finish(parts)


def solution(mesh):
    grid = Mesh(mesh.devices.reshape(NY, NZ, NX, NC), ("y", "z", "x", "c"))
    tm, pair = ("x", "c"), ("y", "z")
    return jax.shard_map(
        body,
        mesh=grid,
        in_specs=(P(tm, None, pair), P(), P(), P(), P()),
        out_specs=P(tm, None, pair, None, None),
        check_vma=False,
    )
```

```python
import jax
import jax.numpy as jnp
import numpy as np
from jax import lax
from jax.experimental import pallas as pl
from jax.experimental.pallas import tpu as pltpu
from jax.sharding import Mesh, PartitionSpec as P

CH = 128
SAMPLES = 2048
NF = 512
BAND = 32
K = 8
R_CH = 64
LAGS = 8
SLOTS = 2
F0 = 64
SEGS = 16
NY, NZ, NX, NC = 4, 16, 4, 2
SEG = 2
SEG_CHIP = SEG * NC
PIECES = NY * NC
CQ = CH // PIECES
FB = 128
NB = NF // FB
KF = 2 * NF
EPS = 1e-06
NORM = np.float32((2.0 * NF * SEGS / SLOTS) ** (-0.5))
BF = jnp.bfloat16
F32 = jnp.float32
VMEM = 48 * 1024 * 1024


def transform_table():
    bins = F0 + np.arange(NF, dtype=np.int64)
    phase = (bins[:, None] * np.arange(SAMPLES // 2, dtype=np.int64)[None, :]) % SAMPLES
    steps = np.arange(SAMPLES, dtype=np.float32) * np.float32(2.0 * np.pi / SAMPLES)
    cos = np.cos(steps)[phase]
    sin = -np.sin(steps)[phase]
    return np.stack([cos, sin], axis=0).astype(jnp.bfloat16)


def lag_tables():
    bins = F0 + np.arange(NF, dtype=np.int64)
    lags = np.arange(LAGS, dtype=np.int64) - LAGS // 2
    phase = (lags[:, None] * bins[None, :]) % SAMPLES
    angle = phase.astype(np.float32) * np.float32(2.0 * np.pi / SAMPLES)
    return np.stack([np.cos(angle), np.sin(angle)], axis=0).astype(np.float32)


def whiten_kernel(traces_hbm, table_hbm, split_ref, low_ref, high_ref, traces_ref, table_ref, trace_sems, table_sems):
    half = SAMPLES // 2
    g = pl.program_id(0)

    def trace_copy(s, h):
        part = pl.ds(h * half, half)
        return pltpu.make_async_copy(traces_hbm.at[s, part], traces_ref.at[s, part], trace_sems.at[s, h])

    def table_copy(b):
        return pltpu.make_async_copy(table_hbm.at[:, pl.ds(b * FB, FB)], table_ref.at[b], table_sems.at[b])

    @pl.when(g == 0)
    def _():
        for s in range(SEG):
            for h in range(2):
                trace_copy(s, h).start()
        for b in range(NB):
            table_copy(b).start()
        for s in range(SEG):
            for h in range(2):
                trace_copy(s, h).wait()

    table_copy(g).wait()
    table = table_ref[g].reshape(2 * FB, half)
    early = jnp.concatenate([traces_ref[s, :half] for s in range(SEG)], axis=1)
    late = jnp.concatenate([traces_ref[s, half:] for s in range(SEG)], axis=1)
    early = jnp.dot(table, early, preferred_element_type=F32)
    late = jnp.dot(table, late, preferred_element_type=F32)
    odd = lax.broadcasted_iota(jnp.int32, late.shape, 0) % 2 == 1
    spectra = early + jnp.where(odd, -late, late)
    grouped = spectra.reshape(2, FB // BAND, BAND, SEG * CH)
    power = jnp.sum(grouped * grouped, axis=(0, 2)) * (1.0 / (2 * BAND))
    scale = 1.0 / jnp.sqrt(power + EPS)
    whitened = grouped * scale[None, :, None, :]
    flipped = whitened.reshape(2 * FB, SEG * CH).T.astype(BF)
    for s in range(SEG):
        low_ref[s] = flipped[s * CH : s * CH + CH // 2]
        high_ref[s] = flipped[s * CH + CH // 2 : (s + 1) * CH]
        for r in range(PIECES):
            split_ref[r, s] = flipped[s * CH + r * CQ : s * CH + (r + 1) * CQ]


def whiten(traces, table):
    half = jax.ShapeDtypeStruct((SEG, CH // 2, KF), BF)
    half_spec = pl.BlockSpec((SEG, CH // 2, 2 * FB), lambda g: (0, 0, g))
    return pl.pallas_call(
        whiten_kernel,
        grid=(NB,),
        in_specs=[pl.BlockSpec(memory_space=pl.ANY), pl.BlockSpec(memory_space=pl.ANY)],
        out_specs=[
            pl.BlockSpec((PIECES, SEG, CQ, 2 * FB), lambda g: (0, 0, 0, g)),
            half_spec,
            half_spec,
        ],
        out_shape=[jax.ShapeDtypeStruct((PIECES, SEG, CQ, KF), BF), half, half],
        scratch_shapes=[
            pltpu.VMEM((SEG, SAMPLES, CH), BF),
            pltpu.VMEM((NB, 2, FB, SAMPLES // 2), BF),
            pltpu.SemaphoreType.DMA((SEG, 2)),
            pltpu.SemaphoreType.DMA((NB,)),
        ],
        compiler_params=pltpu.CompilerParams(vmem_limit_bytes=61 * 1024 * 1024),
        name="whiten",
    )(traces, table)


def lag_kernel_body(core_ref, window_ref, lag_ref, out_ref):
    for b in range(NB):
        at = b * 2 * FB
        real = window_ref[0, 0, :, at : at + FB].astype(F32)
        imag = window_ref[0, 0, :, at + FB : at + 2 * FB].astype(F32)
        for l in range(0, LAGS, 2):
            reals, imags = [], []
            for m in (l, l + 1):
                cos = lag_ref[0, m : m + 1, b * FB : (b + 1) * FB]
                sin = lag_ref[1, m : m + 1, b * FB : (b + 1) * FB]
                reals.append((cos * real + sin * imag) * NORM)
                imags.append((cos * imag - sin * real) * NORM)
            lanes = slice(l * R_CH, (l + 2) * R_CH)
            out_ref[0, 0, at : at + FB, lanes] = jnp.concatenate(reals, axis=0).T.astype(BF)
            out_ref[0, 0, at + FB : at + 2 * FB, lanes] = jnp.concatenate(imags, axis=0).T.astype(BF)


def lag_kernels(core, windows, lags):
    return pl.pallas_call(
        lag_kernel_body,
        grid_spec=pltpu.PrefetchScalarGridSpec(
            num_scalar_prefetch=1,
            grid=(NY, SEG_CHIP),
            in_specs=[
                pl.BlockSpec((1, 1, R_CH, KF), lambda o, s, core: (o, s, 0, 0)),
                pl.BlockSpec((2, LAGS, NF), lambda o, s, core: (0, 0, 0)),
            ],
            out_specs=pl.BlockSpec(
                (1, 1, KF, LAGS * R_CH),
                lambda o, s, core: (o, lax.rem(s + SEG * core[0], SEG_CHIP), 0, 0),
            ),
        ),
        out_shape=jax.ShapeDtypeStruct((NY, SEG_CHIP, KF, LAGS * R_CH), BF),
        compiler_params=pltpu.CompilerParams(vmem_limit_bytes=VMEM),
        name="lag_kernels",
    )(core, windows, lags)


I_COUNT = 2 * NY * K
I_SLOT = I_COUNT + NY
I_Y = I_SLOT + SEG_CHIP


def correlate_body(info_ref, kernel_ref, *refs):
    sources, out_ref = refs[:K], refs[K]
    o = pl.program_id(0)
    row = lax.broadcasted_iota(jnp.int32, (K * CQ, 1), 0)
    live = (row < info_ref[I_COUNT + o] * CQ).astype(F32)
    totals = [0.0] * SLOTS
    for s in range(SEG_CHIP):
        left = jnp.concatenate([ref[0, s // SEG, 0, s % SEG] for ref in sources], axis=0)
        part = jnp.dot(left, kernel_ref[0, s], preferred_element_type=F32)
        for q in range(SLOTS):
            totals[q] = totals[q] + part * (live * (info_ref[I_SLOT + s] == q).astype(F32))
    for l in range(LAGS):
        both = jnp.concatenate([v[:, l * R_CH : (l + 1) * R_CH] for v in totals], axis=1)
        out_ref[l // NC, 0, l % NC] = both.astype(BF)


def correlate(info, kernels, gathered):
    def source_map(k):
        return lambda o, info: (info[o * K + k], 0, info[NY * K + o * K + k], 0, 0, 0)

    return pl.pallas_call(
        correlate_body,
        grid_spec=pltpu.PrefetchScalarGridSpec(
            num_scalar_prefetch=1,
            grid=(NY,),
            in_specs=[
                pl.BlockSpec(
                    (1, SEG_CHIP, KF, LAGS * R_CH),
                    lambda o, info: (lax.rem(info[I_Y] + NY - o, NY), 0, 0, 0),
                )
            ]
            + [pl.BlockSpec((1, NC, 1, SEG, CQ, KF), source_map(k)) for k in range(K)],
            out_specs=pl.BlockSpec((NX, 1, NC, K * CQ, SLOTS * R_CH), lambda o, info: (0, o, 0, 0, 0)),
        ),
        out_shape=jax.ShapeDtypeStruct((NX, NY, NC, K * CQ, SLOTS * R_CH), BF),
        compiler_params=pltpu.CompilerParams(vmem_limit_bytes=VMEM),
        name="correlate",
    )(info, kernels, *([gathered] * K))


def finish_body(parts_ref, out_ref):
    pieces = []
    for c in range(NC):
        for y in range(NY):
            total = parts_ref[y * NC + c].astype(F32)
            for x in range(1, NX):
                total = total + parts_ref[(x * NY + y) * NC + c].astype(F32)
            pieces.append(total)
    for k in range(K):
        rows = jnp.concatenate([v[k * CQ : (k + 1) * CQ] for v in pieces], axis=0).T.astype(BF)
        for q in range(SLOTS):
            out_ref[0, q, k] = rows[q * R_CH : (q + 1) * R_CH]


def finish(parts):
    return pl.pallas_call(
        finish_body,
        out_shape=jax.ShapeDtypeStruct((1, SLOTS, K, R_CH, CH), BF),
        compiler_params=pltpu.CompilerParams(vmem_limit_bytes=VMEM),
        name="finish",
    )(parts)


def body(traces, source_list, source_count, receiver_start, segment_slot):
    y = lax.axis_index("y")
    z = lax.axis_index("z")
    table = jnp.asarray(transform_table())
    lags = jnp.asarray(lag_tables())
    split, low, high = whiten(traces, table)
    crossed = lax.all_to_all(split, ("c", "y"), 0, 0).reshape(NC, NY, SEG, CQ, KF)
    gathered = lax.all_gather(crossed, "z", axis=0, tiled=False)

    low, high, _ = lax.optimization_barrier((low, high, crossed))
    pairs = NY * NZ
    following = lax.ppermute(low, ("y", "z"), [(p, p - 1) for p in range(1, pairs)])
    joined = jnp.concatenate([high, following], axis=1)
    offset = lax.dynamic_index_in_dim(receiver_start, y * NZ + z, keepdims=False) - CH // 2
    window = lax.dynamic_slice_in_dim(joined, offset, R_CH, 1)
    own = jnp.stack(
        [window] + [lax.ppermute(window, "y", [(i, (i + d) % NY) for i in range(NY)]) for d in range(1, NY)]
    )
    other = lax.ppermute(own, "c", [(0, 1), (1, 0)])
    core = lax.axis_index("c")[None].astype(jnp.int32)
    kernels = lag_kernels(core, jnp.concatenate([own, other], axis=1), lags)

    lists = lax.dynamic_index_in_dim(source_list.reshape(NY, NZ, K), z, 1, keepdims=False).reshape(-1)
    counts = lax.dynamic_index_in_dim(source_count.reshape(NY, NZ), z, 1, keepdims=False)
    slots = lax.dynamic_slice_in_dim(segment_slot, lax.axis_index("x") * SEG_CHIP, SEG_CHIP, 0)
    info = jnp.concatenate([lists % NZ, lists // NZ, counts, slots, y[None].astype(jnp.int32)])
    sums = correlate(info, kernels, gathered)
    parts = lax.all_to_all(sums.reshape(NY * LAGS, K * CQ, SLOTS * R_CH), ("x", "y", "c"), 0, 0)
    return finish(parts)


def solution(mesh):
    grid = Mesh(mesh.devices.reshape(NY, NZ, NX, NC), ("y", "z", "x", "c"))
    tm, pair = ("x", "c"), ("y", "z")
    return jax.shard_map(
        body,
        mesh=grid,
        in_specs=(P(tm, None, pair), P(), P(), P(), P()),
        out_specs=P(tm, None, pair, None, None),
        check_vma=False,
    )
```

```python
import jax
import jax.numpy as jnp
import numpy as np
from jax import lax
from jax.experimental import pallas as pl
from jax.experimental.pallas import tpu as pltpu
from jax.sharding import Mesh, PartitionSpec as P

CH = 128
SAMPLES = 2048
NF = 512
BAND = 32
K = 8
R_CH = 64
LAGS = 8
SLOTS = 2
F0 = 64
SEGS = 16
NY, NZ, NX, NC = 4, 16, 4, 2
SEG = 2
SEG_CHIP = SEG * NC
EVEN = LAGS // NC
PIECES = NY * NC
CQ = CH // PIECES
FB = 128
NB = NF // FB
KF = 2 * NF
EPS = 1e-06
NORM = np.float32((2.0 * NF * SEGS / SLOTS) ** (-0.5))
BF = jnp.bfloat16
F32 = jnp.float32
VMEM = 48 * 1024 * 1024


def transform_table():
    bins = F0 + np.arange(NF, dtype=np.int64)
    phase = (bins[:, None] * np.arange(SAMPLES // 2, dtype=np.int64)[None, :]) % SAMPLES
    steps = np.arange(SAMPLES, dtype=np.float32) * np.float32(2.0 * np.pi / SAMPLES)
    cos = np.cos(steps)[phase]
    sin = -np.sin(steps)[phase]
    return np.stack([cos, sin], axis=0).astype(jnp.bfloat16)


def lag_tables():
    bins = F0 + np.arange(NF, dtype=np.int64)
    lags = np.arange(LAGS, dtype=np.int64) - LAGS // 2
    phase = (lags[:, None] * bins[None, :]) % SAMPLES
    angle = phase.astype(np.float32) * np.float32(2.0 * np.pi / SAMPLES)
    return np.stack([np.cos(angle), np.sin(angle)], axis=0).astype(np.float32)


def whiten_kernel(traces_hbm, table_hbm, split_ref, low_ref, high_ref, traces_ref, table_ref, trace_sems, table_sems):
    half = SAMPLES // 2
    g = pl.program_id(0)

    def trace_copy(s, h):
        part = pl.ds(h * half, half)
        return pltpu.make_async_copy(traces_hbm.at[s, part], traces_ref.at[s, part], trace_sems.at[s, h])

    def table_copy(b):
        return pltpu.make_async_copy(table_hbm.at[:, pl.ds(b * FB, FB)], table_ref.at[b], table_sems.at[b])

    @pl.when(g == 0)
    def _():
        for s in range(SEG):
            for h in range(2):
                trace_copy(s, h).start()
        for b in range(NB):
            table_copy(b).start()
        for s in range(SEG):
            for h in range(2):
                trace_copy(s, h).wait()

    table_copy(g).wait()
    table = table_ref[g].reshape(2 * FB, half)
    early = jnp.concatenate([traces_ref[s, :half] for s in range(SEG)], axis=1)
    late = jnp.concatenate([traces_ref[s, half:] for s in range(SEG)], axis=1)
    early = jnp.dot(table, early, preferred_element_type=F32)
    late = jnp.dot(table, late, preferred_element_type=F32)
    odd = lax.broadcasted_iota(jnp.int32, late.shape, 0) % 2 == 1
    spectra = early + jnp.where(odd, -late, late)
    grouped = spectra.reshape(2, FB // BAND, BAND, SEG * CH)
    power = jnp.sum(grouped * grouped, axis=(0, 2)) * (1.0 / (2 * BAND))
    scale = 1.0 / jnp.sqrt(power + EPS)
    whitened = grouped * scale[None, :, None, :]
    flipped = whitened.reshape(2 * FB, SEG * CH).T.astype(BF)
    for s in range(SEG):
        low_ref[s] = flipped[s * CH : s * CH + CH // 2]
        high_ref[s] = flipped[s * CH + CH // 2 : (s + 1) * CH]
        for r in range(PIECES):
            split_ref[r, s] = flipped[s * CH + r * CQ : s * CH + (r + 1) * CQ]


def whiten(traces, table):
    half = jax.ShapeDtypeStruct((SEG, CH // 2, KF), BF)
    half_spec = pl.BlockSpec((SEG, CH // 2, 2 * FB), lambda g: (0, 0, g))
    return pl.pallas_call(
        whiten_kernel,
        grid=(NB,),
        in_specs=[pl.BlockSpec(memory_space=pl.ANY), pl.BlockSpec(memory_space=pl.ANY)],
        out_specs=[
            pl.BlockSpec((PIECES, SEG, CQ, 2 * FB), lambda g: (0, 0, 0, g)),
            half_spec,
            half_spec,
        ],
        out_shape=[jax.ShapeDtypeStruct((PIECES, SEG, CQ, KF), BF), half, half],
        scratch_shapes=[
            pltpu.VMEM((SEG, SAMPLES, CH), BF),
            pltpu.VMEM((NB, 2, FB, SAMPLES // 2), BF),
            pltpu.SemaphoreType.DMA((SEG, 2)),
            pltpu.SemaphoreType.DMA((NB,)),
        ],
        compiler_params=pltpu.CompilerParams(vmem_limit_bytes=61 * 1024 * 1024),
        name="whiten",
    )(traces, table)


def lag_kernel_body(core_ref, window_ref, lag_ref, out_ref):
    for b in range(NB):
        at = b * 2 * FB
        real = window_ref[0, 0, :, at : at + FB].astype(F32)
        imag = window_ref[0, 0, :, at + FB : at + 2 * FB].astype(F32)
        for a in range(0, EVEN, 2):
            reals, imags = [], []
            for m in (NC * a, NC * a + NC):
                cos = lag_ref[0, m : m + 1, b * FB : (b + 1) * FB]
                sin = lag_ref[1, m : m + 1, b * FB : (b + 1) * FB]
                reals.append((cos * real + sin * imag) * NORM)
                imags.append((cos * imag - sin * real) * NORM)
            lanes = slice(a * R_CH, (a + 2) * R_CH)
            out_ref[0, 0, at : at + FB, lanes] = jnp.concatenate(reals, axis=0).T.astype(BF)
            out_ref[0, 0, at + FB : at + 2 * FB, lanes] = jnp.concatenate(imags, axis=0).T.astype(BF)


def lag_kernels(core, windows, lags):
    return pl.pallas_call(
        lag_kernel_body,
        grid_spec=pltpu.PrefetchScalarGridSpec(
            num_scalar_prefetch=1,
            grid=(NY, SEG_CHIP),
            in_specs=[
                pl.BlockSpec((1, 1, R_CH, KF), lambda o, s, core: (o, s, 0, 0)),
                pl.BlockSpec((2, LAGS, NF), lambda o, s, core: (0, 0, 0)),
            ],
            out_specs=pl.BlockSpec(
                (1, 1, KF, EVEN * R_CH),
                lambda o, s, core: (o, lax.rem(s + SEG * core[0], SEG_CHIP), 0, 0),
            ),
        ),
        out_shape=jax.ShapeDtypeStruct((NY, SEG_CHIP, KF, EVEN * R_CH), BF),
        compiler_params=pltpu.CompilerParams(vmem_limit_bytes=VMEM),
        name="lag_kernels",
    )(core, windows, lags)


I_COUNT = 2 * NY * K
I_SLOT = I_COUNT + NY
I_Y = I_SLOT + SEG_CHIP


def turned(rows, lag_ref):
    one = LAGS // 2 + 1
    blocks = []
    for b in range(NB):
        at = b * 2 * FB
        real = rows[:, at : at + FB].astype(F32)
        imag = rows[:, at + FB : at + 2 * FB].astype(F32)
        cos = lag_ref[0, one : one + 1, b * FB : (b + 1) * FB]
        sin = lag_ref[1, one : one + 1, b * FB : (b + 1) * FB]
        blocks.append((real * cos - imag * sin).astype(BF))
        blocks.append((real * sin + imag * cos).astype(BF))
    return jnp.concatenate(blocks, axis=1)


def correlate_body(info_ref, kernel_ref, lag_ref, *refs):
    sources, out_ref = refs[:K], refs[K]
    o = pl.program_id(0)
    row = lax.broadcasted_iota(jnp.int32, (NC * K * CQ, 1), 0) % (K * CQ)
    live = (row < info_ref[I_COUNT + o] * CQ).astype(F32)
    totals = [0.0] * SLOTS
    for s in range(SEG_CHIP):
        rows = jnp.concatenate([ref[0, s // SEG, 0, s % SEG] for ref in sources], axis=0)
        left = jnp.concatenate([rows, turned(rows, lag_ref)], axis=0)
        part = jnp.dot(left, kernel_ref[0, s], preferred_element_type=F32)
        for q in range(SLOTS):
            totals[q] = totals[q] + part * (live * (info_ref[I_SLOT + s] == q).astype(F32))
    for a in range(EVEN):
        for b in range(NC):
            block = [v[b * K * CQ : (b + 1) * K * CQ, a * R_CH : (a + 1) * R_CH] for v in totals]
            out_ref[a, 0, b] = jnp.concatenate(block, axis=1).astype(BF)


def correlate(info, kernels, lags, gathered):
    def source_map(k):
        return lambda o, info: (info[o * K + k], 0, info[NY * K + o * K + k], 0, 0, 0)

    return pl.pallas_call(
        correlate_body,
        grid_spec=pltpu.PrefetchScalarGridSpec(
            num_scalar_prefetch=1,
            grid=(NY,),
            in_specs=[
                pl.BlockSpec(
                    (1, SEG_CHIP, KF, EVEN * R_CH),
                    lambda o, info: (lax.rem(info[I_Y] + NY - o, NY), 0, 0, 0),
                ),
                pl.BlockSpec((2, LAGS, NF), lambda o, info: (0, 0, 0)),
            ]
            + [pl.BlockSpec((1, NC, 1, SEG, CQ, KF), source_map(k)) for k in range(K)],
            out_specs=pl.BlockSpec((NX, 1, NC, K * CQ, SLOTS * R_CH), lambda o, info: (0, o, 0, 0, 0)),
        ),
        out_shape=jax.ShapeDtypeStruct((NX, NY, NC, K * CQ, SLOTS * R_CH), BF),
        compiler_params=pltpu.CompilerParams(vmem_limit_bytes=VMEM),
        name="correlate",
    )(info, kernels, lags, *([gathered] * K))


def finish_body(parts_ref, out_ref):
    pieces = []
    for c in range(NC):
        for y in range(NY):
            total = parts_ref[y * NC + c].astype(F32)
            for x in range(1, NX):
                total = total + parts_ref[(x * NY + y) * NC + c].astype(F32)
            pieces.append(total)
    for k in range(K):
        rows = jnp.concatenate([v[k * CQ : (k + 1) * CQ] for v in pieces], axis=0).T.astype(BF)
        for q in range(SLOTS):
            out_ref[0, q, k] = rows[q * R_CH : (q + 1) * R_CH]


def finish(parts):
    return pl.pallas_call(
        finish_body,
        out_shape=jax.ShapeDtypeStruct((1, SLOTS, K, R_CH, CH), BF),
        compiler_params=pltpu.CompilerParams(vmem_limit_bytes=VMEM),
        name="finish",
    )(parts)


def body(traces, source_list, source_count, receiver_start, segment_slot):
    y = lax.axis_index("y")
    z = lax.axis_index("z")
    table = jnp.asarray(transform_table())
    lags = jnp.asarray(lag_tables())
    split, low, high = whiten(traces, table)
    crossed = lax.all_to_all(split, ("c", "y"), 0, 0).reshape(NC, NY, SEG, CQ, KF)
    gathered = lax.all_gather(crossed, "z", axis=0, tiled=False)

    low, high, _ = lax.optimization_barrier((low, high, crossed))
    pairs = NY * NZ
    following = lax.ppermute(low, ("y", "z"), [(p, p - 1) for p in range(1, pairs)])
    joined = jnp.concatenate([high, following], axis=1)
    offset = lax.dynamic_index_in_dim(receiver_start, y * NZ + z, keepdims=False) - CH // 2
    window = lax.dynamic_slice_in_dim(joined, offset, R_CH, 1)
    own = jnp.stack(
        [window] + [lax.ppermute(window, "y", [(i, (i + d) % NY) for i in range(NY)]) for d in range(1, NY)]
    )
    other = lax.ppermute(own, "c", [(0, 1), (1, 0)])
    core = lax.axis_index("c")[None].astype(jnp.int32)
    kernels = lag_kernels(core, jnp.concatenate([own, other], axis=1), lags)

    lists = lax.dynamic_index_in_dim(source_list.reshape(NY, NZ, K), z, 1, keepdims=False).reshape(-1)
    counts = lax.dynamic_index_in_dim(source_count.reshape(NY, NZ), z, 1, keepdims=False)
    slots = lax.dynamic_slice_in_dim(segment_slot, lax.axis_index("x") * SEG_CHIP, SEG_CHIP, 0)
    info = jnp.concatenate([lists % NZ, lists // NZ, counts, slots, y[None].astype(jnp.int32)])
    sums = correlate(info, kernels, lags, gathered)
    parts = lax.all_to_all(sums.reshape(NY * LAGS, K * CQ, SLOTS * R_CH), ("x", "y", "c"), 0, 0)
    return finish(parts)


def solution(mesh):
    grid = Mesh(mesh.devices.reshape(NY, NZ, NX, NC), ("y", "z", "x", "c"))
    tm, pair = ("x", "c"), ("y", "z")
    return jax.shard_map(
        body,
        mesh=grid,
        in_specs=(P(tm, None, pair), P(), P(), P(), P()),
        out_specs=P(tm, None, pair, None, None),
        check_vma=False,
    )
```

```python
import jax
import jax.numpy as jnp
import numpy as np
from jax import lax
from jax.experimental import pallas as pl
from jax.experimental.pallas import tpu as pltpu
from jax.sharding import Mesh, PartitionSpec as P

CH = 128
SAMPLES = 2048
NF = 512
BAND = 32
K = 8
R_CH = 64
LAGS = 8
SLOTS = 2
F0 = 64
SEGS = 16
NY, NZ, NX, NC = 4, 16, 4, 2
NP = 2
NO = NX // NP
SEG = 2
SEG_PAIR = SEG * NC * NP
EVEN = LAGS // NC
PIECES = NY * NC * NP
CQ = CH // PIECES
FB = 128
NB = NF // FB
KF = 2 * NF
EPS = 1e-06
NORM = np.float32((2.0 * NF * SEGS / SLOTS) ** (-0.5))
BF = jnp.bfloat16
F32 = jnp.float32
VMEM = 48 * 1024 * 1024


def transform_table():
    bins = F0 + np.arange(NF, dtype=np.int64)
    phase = (bins[:, None] * np.arange(SAMPLES // 2, dtype=np.int64)[None, :]) % SAMPLES
    steps = np.arange(SAMPLES, dtype=np.float32) * np.float32(2.0 * np.pi / SAMPLES)
    cos = np.cos(steps)[phase]
    sin = -np.sin(steps)[phase]
    return np.stack([cos, sin], axis=0).astype(jnp.bfloat16)


def lag_tables():
    bins = F0 + np.arange(NF, dtype=np.int64)
    lags = np.arange(LAGS, dtype=np.int64) - LAGS // 2
    phase = (lags[:, None] * bins[None, :]) % SAMPLES
    angle = phase.astype(np.float32) * np.float32(2.0 * np.pi / SAMPLES)
    return np.stack([np.cos(angle), np.sin(angle)], axis=0).astype(np.float32)


def whiten_kernel(traces_hbm, table_hbm, split_ref, low_ref, high_ref, traces_ref, table_ref, trace_sems, table_sems):
    half = SAMPLES // 2
    g = pl.program_id(0)

    def trace_copy(s, h):
        part = pl.ds(h * half, half)
        return pltpu.make_async_copy(traces_hbm.at[s, part], traces_ref.at[s, part], trace_sems.at[s, h])

    def table_copy(b):
        return pltpu.make_async_copy(table_hbm.at[:, pl.ds(b * FB, FB)], table_ref.at[b], table_sems.at[b])

    @pl.when(g == 0)
    def _():
        for s in range(SEG):
            for h in range(2):
                trace_copy(s, h).start()
        for b in range(NB):
            table_copy(b).start()
        for s in range(SEG):
            for h in range(2):
                trace_copy(s, h).wait()

    table_copy(g).wait()
    table = table_ref[g].reshape(2 * FB, half)
    early = jnp.concatenate([traces_ref[s, :half] for s in range(SEG)], axis=1)
    late = jnp.concatenate([traces_ref[s, half:] for s in range(SEG)], axis=1)
    early = jnp.dot(table, early, preferred_element_type=F32)
    late = jnp.dot(table, late, preferred_element_type=F32)
    odd = lax.broadcasted_iota(jnp.int32, late.shape, 0) % 2 == 1
    spectra = early + jnp.where(odd, -late, late)
    grouped = spectra.reshape(2, FB // BAND, BAND, SEG * CH)
    power = jnp.sum(grouped * grouped, axis=(0, 2)) * (1.0 / (2 * BAND))
    scale = 1.0 / jnp.sqrt(power + EPS)
    whitened = grouped * scale[None, :, None, :]
    flipped = whitened.reshape(2 * FB, SEG * CH).T
    for s in range(SEG):
        low_ref[s] = flipped[s * CH : s * CH + CH // 2].astype(BF)
        high_ref[s] = flipped[s * CH + CH // 2 : (s + 1) * CH].astype(BF)
        for r in range(PIECES):
            split_ref[r, s] = flipped[s * CH + r * CQ : s * CH + (r + 1) * CQ].astype(BF)


def whiten(traces, table):
    half = jax.ShapeDtypeStruct((SEG, CH // 2, KF), BF)
    half_spec = pl.BlockSpec((SEG, CH // 2, 2 * FB), lambda g: (0, 0, g))
    return pl.pallas_call(
        whiten_kernel,
        grid=(NB,),
        in_specs=[pl.BlockSpec(memory_space=pl.ANY), pl.BlockSpec(memory_space=pl.ANY)],
        out_specs=[
            pl.BlockSpec((PIECES, SEG, CQ, 2 * FB), lambda g: (0, 0, 0, g)),
            half_spec,
            half_spec,
        ],
        out_shape=[jax.ShapeDtypeStruct((PIECES, SEG, CQ, KF), BF), half, half],
        scratch_shapes=[
            pltpu.VMEM((SEG, SAMPLES, CH), BF),
            pltpu.VMEM((NB, 2, FB, SAMPLES // 2), BF),
            pltpu.SemaphoreType.DMA((SEG, 2)),
            pltpu.SemaphoreType.DMA((NB,)),
        ],
        compiler_params=pltpu.CompilerParams(vmem_limit_bytes=61 * 1024 * 1024),
        name="whiten",
    )(traces, table)


def lag_kernel_body(core_ref, window_ref, lag_ref, out_ref):
    for b in range(NB):
        at = b * 2 * FB
        real = window_ref[0, 0, :, at : at + FB].astype(F32)
        imag = window_ref[0, 0, :, at + FB : at + 2 * FB].astype(F32)
        for a in range(0, EVEN, 2):
            reals, imags = [], []
            for m in (NC * a, NC * a + NC):
                cos = lag_ref[0, m : m + 1, b * FB : (b + 1) * FB]
                sin = lag_ref[1, m : m + 1, b * FB : (b + 1) * FB]
                reals.append((cos * real + sin * imag) * NORM)
                imags.append((cos * imag - sin * real) * NORM)
            lanes = slice(a * R_CH, (a + 2) * R_CH)
            out_ref[0, 0, at : at + FB, lanes] = jnp.concatenate(reals, axis=0).T.astype(BF)
            out_ref[0, 0, at + FB : at + 2 * FB, lanes] = jnp.concatenate(imags, axis=0).T.astype(BF)


def segment_place(s, core):
    half = SEG * NC
    chip = lax.rem(s // half + core[1], NP)
    return chip * half + lax.rem(lax.rem(s, half) + SEG * core[0], half)


def lag_kernels(core, windows, lags):
    return pl.pallas_call(
        lag_kernel_body,
        grid_spec=pltpu.PrefetchScalarGridSpec(
            num_scalar_prefetch=1,
            grid=(NY, SEG_PAIR),
            in_specs=[
                pl.BlockSpec((1, 1, R_CH, KF), lambda o, s, core: (o, s, 0, 0)),
                pl.BlockSpec((2, LAGS, NF), lambda o, s, core: (0, 0, 0)),
            ],
            out_specs=pl.BlockSpec(
                (1, 1, KF, EVEN * R_CH),
                lambda o, s, core: (o, segment_place(s, core), 0, 0),
            ),
        ),
        out_shape=jax.ShapeDtypeStruct((NY, SEG_PAIR, KF, EVEN * R_CH), BF),
        compiler_params=pltpu.CompilerParams(vmem_limit_bytes=VMEM),
        name="lag_kernels",
    )(core, windows, lags)


I_COUNT = 2 * NY * K
I_SLOT = I_COUNT + NY
I_Y = I_SLOT + SEG_PAIR


def turned(rows, lag_ref):
    one = LAGS // 2 + 1
    blocks = []
    for b in range(NB):
        at = b * 2 * FB
        real = rows[:, at : at + FB].astype(F32)
        imag = rows[:, at + FB : at + 2 * FB].astype(F32)
        cos = lag_ref[0, one : one + 1, b * FB : (b + 1) * FB]
        sin = lag_ref[1, one : one + 1, b * FB : (b + 1) * FB]
        blocks.append((real * cos - imag * sin).astype(BF))
        blocks.append((real * sin + imag * cos).astype(BF))
    return jnp.concatenate(blocks, axis=1)


def correlate_body(info_ref, kernel_ref, lag_ref, *refs):
    sources, out_ref = refs[:K], refs[K]
    o = pl.program_id(0)
    row = lax.broadcasted_iota(jnp.int32, (NC * K * CQ, 1), 0) % (K * CQ)
    live = (row < info_ref[I_COUNT + o] * CQ).astype(F32)
    totals = [0.0] * SLOTS
    for s in range(SEG_PAIR):
        at = (0, s // (SEG * NC), s // SEG % NC, 0, s % SEG)
        rows = jnp.concatenate([ref[at].astype(F32) for ref in sources], axis=0).astype(BF)
        left = jnp.concatenate([rows, turned(rows, lag_ref)], axis=0)
        part = jnp.dot(left, kernel_ref[0, s], preferred_element_type=F32)
        for q in range(SLOTS):
            totals[q] = totals[q] + part * (live * (info_ref[I_SLOT + s] == q).astype(F32))
    for a in range(EVEN):
        for b in range(NC):
            block = [v[b * K * CQ : (b + 1) * K * CQ, a * R_CH : (a + 1) * R_CH] for v in totals]
            out_ref[a, 0, b] = jnp.concatenate(block, axis=1).astype(BF)


def correlate(info, kernels, lags, gathered):
    def source_map(k):
        return lambda o, info: (info[o * K + k], 0, 0, info[NY * K + o * K + k], 0, 0, 0)

    return pl.pallas_call(
        correlate_body,
        grid_spec=pltpu.PrefetchScalarGridSpec(
            num_scalar_prefetch=1,
            grid=(NY,),
            in_specs=[
                pl.BlockSpec(
                    (1, SEG_PAIR, KF, EVEN * R_CH),
                    lambda o, info: (lax.rem(info[I_Y] + NY - o, NY), 0, 0, 0),
                ),
                pl.BlockSpec((2, LAGS, NF), lambda o, info: (0, 0, 0)),
            ]
            + [pl.BlockSpec((1, NP, NC, 1, SEG, CQ, KF), source_map(k)) for k in range(K)],
            out_specs=pl.BlockSpec((NX, 1, NC, K * CQ, SLOTS * R_CH), lambda o, info: (0, o, 0, 0, 0)),
        ),
        out_shape=jax.ShapeDtypeStruct((NX, NY, NC, K * CQ, SLOTS * R_CH), BF),
        compiler_params=pltpu.CompilerParams(vmem_limit_bytes=VMEM),
        name="correlate",
    )(info, kernels, lags, *([gathered] * K))


def finish_body(parts_ref, out_ref):
    pieces = []
    for p in range(NP):
        for c in range(NC):
            for y in range(NY):
                total = parts_ref[(p * NY + y) * NC + c].astype(F32)
                for x in range(1, NO):
                    total = total + parts_ref[((x * NP + p) * NY + y) * NC + c].astype(F32)
                pieces.append(total)
    for k in range(K):
        rows = jnp.concatenate([v[k * CQ : (k + 1) * CQ] for v in pieces], axis=0).T.astype(BF)
        for q in range(SLOTS):
            out_ref[0, q, k] = rows[q * R_CH : (q + 1) * R_CH]


def finish(parts):
    return pl.pallas_call(
        finish_body,
        out_shape=jax.ShapeDtypeStruct((1, SLOTS, K, R_CH, CH), BF),
        compiler_params=pltpu.CompilerParams(vmem_limit_bytes=VMEM),
        name="finish",
    )(parts)


def body(traces, source_list, source_count, receiver_start, segment_slot):
    y = lax.axis_index("y")
    z = lax.axis_index("z")
    table = jnp.asarray(transform_table())
    lags = jnp.asarray(lag_tables())
    split, low, high = whiten(traces, table)
    crossed = lax.all_to_all(split, ("xl", "c", "y"), 0, 0).reshape(NP, NC, NY, SEG, CQ, KF)
    gathered = lax.all_gather(crossed, "z", axis=0, tiled=False)

    low, high, _ = lax.optimization_barrier((low, high, crossed))
    pairs = NY * NZ
    following = lax.ppermute(low, ("y", "z"), [(p, p - 1) for p in range(1, pairs)])
    joined = jnp.concatenate([high, following], axis=1)
    offset = lax.dynamic_index_in_dim(receiver_start, y * NZ + z, keepdims=False) - CH // 2
    window = lax.dynamic_slice_in_dim(joined, offset, R_CH, 1)
    own = jnp.stack(
        [window] + [lax.ppermute(window, "y", [(i, (i + d) % NY) for i in range(NY)]) for d in range(1, NY)]
    )
    other = lax.ppermute(own, "c", [(0, 1), (1, 0)])
    chip = jnp.concatenate([own, other], axis=1)
    beside = lax.ppermute(chip, "xl", [(0, 1), (1, 0)])
    core = jnp.stack([lax.axis_index("c"), lax.axis_index("xl")]).astype(jnp.int32)
    kernels = lag_kernels(core, jnp.concatenate([chip, beside], axis=1), lags)

    lists = lax.dynamic_index_in_dim(source_list.reshape(NY, NZ, K), z, 1, keepdims=False).reshape(-1)
    counts = lax.dynamic_index_in_dim(source_count.reshape(NY, NZ), z, 1, keepdims=False)
    slots = lax.dynamic_slice_in_dim(segment_slot, lax.axis_index("xh") * SEG_PAIR, SEG_PAIR, 0)
    info = jnp.concatenate([lists % NZ, lists // NZ, counts, slots, y[None].astype(jnp.int32)])
    sums = correlate(info, kernels, lags, gathered)
    parts = lax.all_to_all(sums.reshape(NY * LAGS, K * CQ, SLOTS * R_CH), ("xh", "xl", "y", "c"), 0, 0)
    return finish(parts)


def solution(mesh):
    grid = Mesh(mesh.devices.reshape(NY, NZ, NO, NP, NC), ("y", "z", "xh", "xl", "c"))
    tm, pair = ("xh", "xl", "c"), ("y", "z")
    return jax.shard_map(
        body,
        mesh=grid,
        in_specs=(P(tm, None, pair), P(), P(), P(), P()),
        out_specs=P(tm, None, pair, None, None),
        check_vma=False,
    )
```

```python
import jax
import jax.numpy as jnp
import numpy as np
from jax import lax
from jax.experimental import pallas as pl
from jax.experimental.pallas import tpu as pltpu
from jax.sharding import Mesh, PartitionSpec as P

CH = 128
SAMPLES = 2048
NF = 512
BAND = 32
K = 8
R_CH = 64
LAGS = 8
SLOTS = 2
F0 = 64
SEGS = 16
NY, NZ, NX, NC = 4, 16, 4, 2
NP = 2
NO = NX // NP
SEG = 2
SEG_PAIR = SEG * NC * NP
EVEN = LAGS // NC
PIECES = NY * NC * NP
CQ = CH // PIECES
FB = 128
NB = NF // FB
KF = 2 * NF
EPS = 1e-06
NORM = np.float32((2.0 * NF * SEGS / SLOTS) ** (-0.5))
BF = jnp.bfloat16
F32 = jnp.float32
VMEM = 48 * 1024 * 1024


def transform_table():
    bins = F0 + np.arange(NF, dtype=np.int64)
    phase = (bins[:, None] * np.arange(SAMPLES // 2, dtype=np.int64)[None, :]) % SAMPLES
    steps = np.arange(SAMPLES, dtype=np.float32) * np.float32(2.0 * np.pi / SAMPLES)
    cos = np.cos(steps)[phase]
    sin = -np.sin(steps)[phase]
    return np.stack([cos, sin], axis=0).astype(jnp.bfloat16)


def lag_tables():
    bins = F0 + np.arange(NF, dtype=np.int64)
    lags = np.arange(LAGS, dtype=np.int64) - LAGS // 2
    phase = (lags[:, None] * bins[None, :]) % SAMPLES
    angle = phase.astype(np.float32) * np.float32(2.0 * np.pi / SAMPLES)
    return np.stack([np.cos(angle), np.sin(angle)], axis=0).astype(np.float32)


def whiten_kernel(traces_hbm, table_hbm, split_ref, low_ref, high_ref, traces_ref, table_ref, trace_sems, table_sems):
    half = SAMPLES // 2
    g = pl.program_id(0)

    def trace_copy(s, h):
        part = pl.ds(h * half, half)
        return pltpu.make_async_copy(traces_hbm.at[s, part], traces_ref.at[s, part], trace_sems.at[s, h])

    def table_copy(b):
        return pltpu.make_async_copy(table_hbm.at[:, pl.ds(b * FB, FB)], table_ref.at[b], table_sems.at[b])

    @pl.when(g == 0)
    def _():
        for s in range(SEG):
            for h in range(2):
                trace_copy(s, h).start()
        for b in range(NB):
            table_copy(b).start()
        for s in range(SEG):
            for h in range(2):
                trace_copy(s, h).wait()

    table_copy(g).wait()
    table = table_ref[g].reshape(2 * FB, half)
    early = jnp.concatenate([traces_ref[s, :half] for s in range(SEG)], axis=1)
    late = jnp.concatenate([traces_ref[s, half:] for s in range(SEG)], axis=1)
    early = jnp.dot(table, early, preferred_element_type=F32)
    late = jnp.dot(table, late, preferred_element_type=F32)
    odd = lax.broadcasted_iota(jnp.int32, late.shape, 0) % 2 == 1
    spectra = early + jnp.where(odd, -late, late)
    grouped = spectra.reshape(2, FB // BAND, BAND, SEG * CH)
    power = jnp.sum(grouped * grouped, axis=(0, 2)) * (1.0 / (2 * BAND))
    scale = 1.0 / jnp.sqrt(power + EPS)
    whitened = grouped * scale[None, :, None, :]
    flipped = whitened.reshape(2 * FB, SEG * CH).T
    for s in range(SEG):
        low_ref[s] = flipped[s * CH : s * CH + CH // 2].astype(BF)
        high_ref[s] = flipped[s * CH + CH // 2 : (s + 1) * CH].astype(BF)
        for r in range(PIECES):
            split_ref[r, s] = flipped[s * CH + r * CQ : s * CH + (r + 1) * CQ].astype(BF)


def whiten(traces, table):
    half = jax.ShapeDtypeStruct((SEG, CH // 2, KF), BF)
    half_spec = pl.BlockSpec((SEG, CH // 2, 2 * FB), lambda g: (0, 0, g))
    return pl.pallas_call(
        whiten_kernel,
        grid=(NB,),
        in_specs=[pl.BlockSpec(memory_space=pl.ANY), pl.BlockSpec(memory_space=pl.ANY)],
        out_specs=[
            pl.BlockSpec((PIECES, SEG, CQ, 2 * FB), lambda g: (0, 0, 0, g)),
            half_spec,
            half_spec,
        ],
        out_shape=[jax.ShapeDtypeStruct((PIECES, SEG, CQ, KF), BF), half, half],
        scratch_shapes=[
            pltpu.VMEM((SEG, SAMPLES, CH), BF),
            pltpu.VMEM((NB, 2, FB, SAMPLES // 2), BF),
            pltpu.SemaphoreType.DMA((SEG, 2)),
            pltpu.SemaphoreType.DMA((NB,)),
        ],
        compiler_params=pltpu.CompilerParams(vmem_limit_bytes=61 * 1024 * 1024),
        name="whiten",
    )(traces, table)


def lag_kernel_body(core_ref, window_ref, lag_ref, *refs):
    out_ref = refs[-1]
    for b in range(NB):
        at = b * 2 * FB
        real = window_ref[0, 0, :, at : at + FB].astype(F32)
        imag = window_ref[0, 0, :, at + FB : at + 2 * FB].astype(F32)
        for a in range(0, EVEN, 2):
            reals, imags = [], []
            for m in (NC * a, NC * a + NC):
                cos = lag_ref[0, m : m + 1, b * FB : (b + 1) * FB]
                sin = lag_ref[1, m : m + 1, b * FB : (b + 1) * FB]
                reals.append((cos * real + sin * imag) * NORM)
                imags.append((cos * imag - sin * real) * NORM)
            lanes = slice(a * R_CH, (a + 2) * R_CH)
            out_ref[0, 0, at : at + FB, lanes] = jnp.concatenate(reals, axis=0).T.astype(BF)
            out_ref[0, 0, at + FB : at + 2 * FB, lanes] = jnp.concatenate(imags, axis=0).T.astype(BF)


def segment_place(s, core):
    half = SEG * NC
    chip = lax.rem(s // half + core[1], NP)
    return chip * half + lax.rem(lax.rem(s, half) + SEG * core[0], half)


def lag_kernels(core, windows, lags, first, kernels):
    earlier = [] if kernels is None else [kernels]
    return pl.pallas_call(
        lag_kernel_body,
        grid_spec=pltpu.PrefetchScalarGridSpec(
            num_scalar_prefetch=1,
            grid=(NY, SEG * NC),
            in_specs=[
                pl.BlockSpec((1, 1, R_CH, KF), lambda o, s, core: (o, s, 0, 0)),
                pl.BlockSpec((2, LAGS, NF), lambda o, s, core: (0, 0, 0)),
            ]
            + [pl.BlockSpec(memory_space=pl.ANY)] * len(earlier),
            out_specs=pl.BlockSpec(
                (1, 1, KF, EVEN * R_CH),
                lambda o, s, core: (o, segment_place(s + first, core), 0, 0),
            ),
        ),
        out_shape=jax.ShapeDtypeStruct((NY, SEG_PAIR, KF, EVEN * R_CH), BF),
        input_output_aliases={3: 0} if earlier else {},
        compiler_params=pltpu.CompilerParams(vmem_limit_bytes=VMEM),
        name="lag_kernels",
    )(core, windows, lags, *earlier)


I_COUNT = 2 * NY * K
I_SLOT = I_COUNT + NY
I_Y = I_SLOT + SEG_PAIR


def turned(rows, lag_ref):
    one = LAGS // 2 + 1
    blocks = []
    for b in range(NB):
        at = b * 2 * FB
        real = rows[:, at : at + FB].astype(F32)
        imag = rows[:, at + FB : at + 2 * FB].astype(F32)
        cos = lag_ref[0, one : one + 1, b * FB : (b + 1) * FB]
        sin = lag_ref[1, one : one + 1, b * FB : (b + 1) * FB]
        blocks.append((real * cos - imag * sin).astype(BF))
        blocks.append((real * sin + imag * cos).astype(BF))
    return jnp.concatenate(blocks, axis=1)


def correlate_body(info_ref, kernel_ref, lag_ref, *refs):
    sources, out_ref = refs[:K], refs[K]
    o = pl.program_id(0)
    row = lax.broadcasted_iota(jnp.int32, (NC * K * CQ, 1), 0) % (K * CQ)
    live = (row < info_ref[I_COUNT + o] * CQ).astype(F32)
    totals = [0.0] * SLOTS
    for s in range(SEG_PAIR):
        at = (0, s // (SEG * NC), s // SEG % NC, 0, s % SEG)
        rows = jnp.concatenate([ref[at].astype(F32) for ref in sources], axis=0).astype(BF)
        left = jnp.concatenate([rows, turned(rows, lag_ref)], axis=0)
        part = jnp.dot(left, kernel_ref[0, s], preferred_element_type=F32)
        for q in range(SLOTS):
            totals[q] = totals[q] + part * (live * (info_ref[I_SLOT + s] == q).astype(F32))
    for a in range(EVEN):
        for b in range(NC):
            block = [v[b * K * CQ : (b + 1) * K * CQ, a * R_CH : (a + 1) * R_CH] for v in totals]
            out_ref[a, 0, b] = jnp.concatenate(block, axis=1).astype(BF)


def correlate(info, kernels, lags, gathered):
    def source_map(k):
        return lambda o, info: (info[o * K + k], 0, 0, info[NY * K + o * K + k], 0, 0, 0)

    return pl.pallas_call(
        correlate_body,
        grid_spec=pltpu.PrefetchScalarGridSpec(
            num_scalar_prefetch=1,
            grid=(NY,),
            in_specs=[
                pl.BlockSpec(
                    (1, SEG_PAIR, KF, EVEN * R_CH),
                    lambda o, info: (lax.rem(info[I_Y] + NY - o, NY), 0, 0, 0),
                ),
                pl.BlockSpec((2, LAGS, NF), lambda o, info: (0, 0, 0)),
            ]
            + [pl.BlockSpec((1, NP, NC, 1, SEG, CQ, KF), source_map(k)) for k in range(K)],
            out_specs=pl.BlockSpec((NX, 1, NC, K * CQ, SLOTS * R_CH), lambda o, info: (0, o, 0, 0, 0)),
        ),
        out_shape=jax.ShapeDtypeStruct((NX, NY, NC, K * CQ, SLOTS * R_CH), BF),
        compiler_params=pltpu.CompilerParams(vmem_limit_bytes=VMEM),
        name="correlate",
    )(info, kernels, lags, *([gathered] * K))


def finish_body(parts_ref, out_ref):
    pieces = []
    for p in range(NP):
        for c in range(NC):
            for y in range(NY):
                total = parts_ref[(p * NY + y) * NC + c].astype(F32)
                for x in range(1, NO):
                    total = total + parts_ref[((x * NP + p) * NY + y) * NC + c].astype(F32)
                pieces.append(total)
    for k in range(K):
        rows = jnp.concatenate([v[k * CQ : (k + 1) * CQ] for v in pieces], axis=0).T.astype(BF)
        for q in range(SLOTS):
            out_ref[0, q, k] = rows[q * R_CH : (q + 1) * R_CH]


def finish(parts):
    return pl.pallas_call(
        finish_body,
        out_shape=jax.ShapeDtypeStruct((1, SLOTS, K, R_CH, CH), BF),
        compiler_params=pltpu.CompilerParams(vmem_limit_bytes=VMEM),
        name="finish",
    )(parts)


def body(traces, source_list, source_count, receiver_start, segment_slot):
    y = lax.axis_index("y")
    z = lax.axis_index("z")
    table = jnp.asarray(transform_table())
    lags = jnp.asarray(lag_tables())
    split, low, high = whiten(traces, table)
    crossed = lax.all_to_all(split, ("xl", "c", "y"), 0, 0).reshape(NP, NC, NY, SEG, CQ, KF)
    gathered = lax.all_gather(crossed, "z", axis=0, tiled=False)

    low, high, _ = lax.optimization_barrier((low, high, crossed))
    pairs = NY * NZ
    following = lax.ppermute(low, ("y", "z"), [(p, p - 1) for p in range(1, pairs)])
    joined = jnp.concatenate([high, following], axis=1)
    offset = lax.dynamic_index_in_dim(receiver_start, y * NZ + z, keepdims=False) - CH // 2
    window = lax.dynamic_slice_in_dim(joined, offset, R_CH, 1)
    own = jnp.stack(
        [window] + [lax.ppermute(window, "y", [(i, (i + d) % NY) for i in range(NY)]) for d in range(1, NY)]
    )
    other = lax.ppermute(own, "c", [(0, 1), (1, 0)])
    chip = jnp.concatenate([own, other], axis=1)
    beside = lax.ppermute(chip, "xl", [(0, 1), (1, 0)])
    core = jnp.stack([lax.axis_index("c"), lax.axis_index("xl")]).astype(jnp.int32)
    kernels = lag_kernels(core, chip, lags, 0, None)
    kernels = lag_kernels(core, beside, lags, SEG * NC, kernels)

    lists = lax.dynamic_index_in_dim(source_list.reshape(NY, NZ, K), z, 1, keepdims=False).reshape(-1)
    counts = lax.dynamic_index_in_dim(source_count.reshape(NY, NZ), z, 1, keepdims=False)
    slots = lax.dynamic_slice_in_dim(segment_slot, lax.axis_index("xh") * SEG_PAIR, SEG_PAIR, 0)
    info = jnp.concatenate([lists % NZ, lists // NZ, counts, slots, y[None].astype(jnp.int32)])
    sums = correlate(info, kernels, lags, gathered)
    parts = lax.all_to_all(sums.reshape(NY * LAGS, K * CQ, SLOTS * R_CH), ("xh", "xl", "y", "c"), 0, 0)
    return finish(parts)


def solution(mesh):
    grid = Mesh(mesh.devices.reshape(NY, NZ, NO, NP, NC), ("y", "z", "xh", "xl", "c"))
    tm, pair = ("xh", "xl", "c"), ("y", "z")
    return jax.shard_map(
        body,
        mesh=grid,
        in_specs=(P(tm, None, pair), P(), P(), P(), P()),
        out_specs=P(tm, None, pair, None, None),
        check_vma=False,
    )
```

```python
import jax
import jax.numpy as jnp
import numpy as np
from jax import lax
from jax.experimental import pallas as pl
from jax.experimental.pallas import tpu as pltpu
from jax.sharding import Mesh, PartitionSpec as P

CH = 128
SAMPLES = 2048
NF = 512
BAND = 32
K = 8
R_CH = 64
LAGS = 8
SLOTS = 2
F0 = 64
SEGS = 16
NY, NZ, NX, NC = 4, 16, 4, 2
NP = 2
NO = NX // NP
SEG = 2
SEG_PAIR = SEG * NC * NP
EVEN = LAGS // NC
PIECES = NY * NC * NP
CQ = CH // PIECES
FB = 128
NB = NF // FB
KF = 2 * NF
EPS = 1e-06
NORM = np.float32((2.0 * NF * SEGS / SLOTS) ** (-0.5))
BF = jnp.bfloat16
F32 = jnp.float32
VMEM = 48 * 1024 * 1024


def transform_table():
    bins = F0 + np.arange(NF, dtype=np.int64)
    phase = (bins[:, None] * np.arange(SAMPLES // 2, dtype=np.int64)[None, :]) % SAMPLES
    steps = np.arange(SAMPLES, dtype=np.float32) * np.float32(2.0 * np.pi / SAMPLES)
    cos = np.cos(steps)[phase]
    sin = -np.sin(steps)[phase]
    return np.stack([cos, sin], axis=0).astype(jnp.bfloat16)


def lag_tables():
    bins = F0 + np.arange(NF, dtype=np.int64)
    lags = np.arange(LAGS, dtype=np.int64) - LAGS // 2
    phase = (lags[:, None] * bins[None, :]) % SAMPLES
    angle = phase.astype(np.float32) * np.float32(2.0 * np.pi / SAMPLES)
    return np.stack([np.cos(angle), np.sin(angle)], axis=0).astype(np.float32)


def whiten_kernel(traces_hbm, table_hbm, split_ref, low_ref, high_ref, traces_ref, table_ref, trace_sems, table_sems):
    half = SAMPLES // 2
    g = pl.program_id(0)

    def trace_copy(s, h):
        part = pl.ds(h * half, half)
        return pltpu.make_async_copy(traces_hbm.at[s, part], traces_ref.at[s, part], trace_sems.at[s, h])

    def table_copy(b):
        return pltpu.make_async_copy(table_hbm.at[:, pl.ds(b * FB, FB)], table_ref.at[b], table_sems.at[b])

    @pl.when(g == 0)
    def _():
        for s in range(SEG):
            for h in range(2):
                trace_copy(s, h).start()
        for b in range(NB):
            table_copy(b).start()
        for s in range(SEG):
            for h in range(2):
                trace_copy(s, h).wait()

    table_copy(g).wait()
    table = table_ref[g].reshape(2 * FB, half)
    early = jnp.concatenate([traces_ref[s, :half] for s in range(SEG)], axis=1)
    late = jnp.concatenate([traces_ref[s, half:] for s in range(SEG)], axis=1)
    early = jnp.dot(table, early, preferred_element_type=F32)
    late = jnp.dot(table, late, preferred_element_type=F32)
    odd = lax.broadcasted_iota(jnp.int32, late.shape, 0) % 2 == 1
    spectra = early + jnp.where(odd, -late, late)
    grouped = spectra.reshape(2, FB // BAND, BAND, SEG * CH)
    power = jnp.sum(grouped * grouped, axis=(0, 2)) * (1.0 / (2 * BAND))
    scale = 1.0 / jnp.sqrt(power + EPS)
    whitened = grouped * scale[None, :, None, :]
    flipped = whitened.reshape(2 * FB, SEG * CH).T
    for s in range(SEG):
        low_ref[s] = flipped[s * CH : s * CH + CH // 2].astype(BF)
        high_ref[s] = flipped[s * CH + CH // 2 : (s + 1) * CH].astype(BF)
        for r in range(PIECES):
            split_ref[r, s] = flipped[s * CH + r * CQ : s * CH + (r + 1) * CQ].astype(BF)


def whiten(traces, table):
    half = jax.ShapeDtypeStruct((SEG, CH // 2, KF), BF)
    half_spec = pl.BlockSpec((SEG, CH // 2, 2 * FB), lambda g: (0, 0, g))
    return pl.pallas_call(
        whiten_kernel,
        grid=(NB,),
        in_specs=[pl.BlockSpec(memory_space=pl.ANY), pl.BlockSpec(memory_space=pl.ANY)],
        out_specs=[
            pl.BlockSpec((PIECES, SEG, CQ, 2 * FB), lambda g: (0, 0, 0, g)),
            half_spec,
            half_spec,
        ],
        out_shape=[jax.ShapeDtypeStruct((PIECES, SEG, CQ, KF), BF), half, half],
        scratch_shapes=[
            pltpu.VMEM((SEG, SAMPLES, CH), BF),
            pltpu.VMEM((NB, 2, FB, SAMPLES // 2), BF),
            pltpu.SemaphoreType.DMA((SEG, 2)),
            pltpu.SemaphoreType.DMA((NB,)),
        ],
        compiler_params=pltpu.CompilerParams(vmem_limit_bytes=61 * 1024 * 1024),
        name="whiten",
    )(traces, table)


def lag_kernel_body(core_ref, window_ref, lag_ref, *refs):
    out_ref = refs[-1]
    for b in range(NB):
        at = b * 2 * FB
        real = window_ref[0, 0, :, at : at + FB].astype(F32)
        imag = window_ref[0, 0, :, at + FB : at + 2 * FB].astype(F32)
        for a in range(0, EVEN, 2):
            reals, imags = [], []
            for m in (NC * a, NC * a + NC):
                cos = lag_ref[0, m : m + 1, b * FB : (b + 1) * FB]
                sin = lag_ref[1, m : m + 1, b * FB : (b + 1) * FB]
                reals.append((cos * real + sin * imag) * NORM)
                imags.append((cos * imag - sin * real) * NORM)
            lanes = slice(a * R_CH, (a + 2) * R_CH)
            out_ref[0, 0, at : at + FB, lanes] = jnp.concatenate(reals, axis=0).T.astype(BF)
            out_ref[0, 0, at + FB : at + 2 * FB, lanes] = jnp.concatenate(imags, axis=0).T.astype(BF)


def segment_place(s, core):
    half = SEG * NC
    chip = lax.rem(s // half + core[1], NP)
    return chip * half + lax.rem(lax.rem(s, half) + SEG * core[0], half)


def lag_kernels(core, windows, lags, first, kernels):
    earlier = [] if kernels is None else [kernels]
    return pl.pallas_call(
        lag_kernel_body,
        grid_spec=pltpu.PrefetchScalarGridSpec(
            num_scalar_prefetch=1,
            grid=(NY, SEG * NC),
            in_specs=[
                pl.BlockSpec((1, 1, R_CH, KF), lambda o, s, core: (o, s, 0, 0)),
                pl.BlockSpec((2, LAGS, NF), lambda o, s, core: (0, 0, 0)),
            ]
            + [pl.BlockSpec(memory_space=pl.ANY)] * len(earlier),
            out_specs=pl.BlockSpec(
                (1, 1, KF, EVEN * R_CH),
                lambda o, s, core: (o, segment_place(s + first, core), 0, 0),
            ),
        ),
        out_shape=jax.ShapeDtypeStruct((NY, SEG_PAIR, KF, EVEN * R_CH), BF),
        input_output_aliases={3: 0} if earlier else {},
        compiler_params=pltpu.CompilerParams(vmem_limit_bytes=VMEM),
        name="lag_kernels",
    )(core, windows, lags, *earlier)


I_COUNT = 2 * NY * K
I_SLOT = I_COUNT + NY
I_Y = I_SLOT + SEG_PAIR


def turned(rows, lag_ref):
    one = LAGS // 2 + 1
    blocks = []
    for b in range(NB):
        at = b * 2 * FB
        real = rows[:, at : at + FB].astype(F32)
        imag = rows[:, at + FB : at + 2 * FB].astype(F32)
        cos = lag_ref[0, one : one + 1, b * FB : (b + 1) * FB]
        sin = lag_ref[1, one : one + 1, b * FB : (b + 1) * FB]
        blocks.append((real * cos - imag * sin).astype(BF))
        blocks.append((real * sin + imag * cos).astype(BF))
    return jnp.concatenate(blocks, axis=1)


def correlate_body(info_ref, kernel_ref, lag_ref, *refs):
    sources, out_ref = refs[:K], refs[K]
    o = pl.program_id(0)
    row = lax.broadcasted_iota(jnp.int32, (NC * K * CQ, 1), 0) % (K * CQ)
    live = (row < info_ref[I_COUNT + o] * CQ).astype(F32)
    totals = [0.0] * SLOTS
    for s in range(SEG_PAIR):
        at = (0, s // (SEG * NC), s // SEG % NC, 0, s % SEG)
        rows = jnp.concatenate([ref[at].astype(F32) for ref in sources], axis=0).astype(BF)
        left = jnp.concatenate([rows, turned(rows, lag_ref)], axis=0)
        part = jnp.dot(left, kernel_ref[0, s], preferred_element_type=F32)
        for q in range(SLOTS):
            totals[q] = totals[q] + part * (live * (info_ref[I_SLOT + s] == q).astype(F32))
    for a in range(EVEN):
        for b in range(NC):
            block = [v[b * K * CQ : (b + 1) * K * CQ, a * R_CH : (a + 1) * R_CH] for v in totals]
            out_ref[a, 0, b] = jnp.concatenate(block, axis=1).astype(BF)


def correlate(info, kernels, lags, gathered):
    def source_map(k):
        return lambda o, info: (info[o * K + k], 0, 0, info[NY * K + o * K + k], 0, 0, 0)

    return pl.pallas_call(
        correlate_body,
        grid_spec=pltpu.PrefetchScalarGridSpec(
            num_scalar_prefetch=1,
            grid=(NY,),
            in_specs=[
                pl.BlockSpec(
                    (1, SEG_PAIR, KF, EVEN * R_CH),
                    lambda o, info: (lax.rem(info[I_Y] + NY - o, NY), 0, 0, 0),
                ),
                pl.BlockSpec((2, LAGS, NF), lambda o, info: (0, 0, 0)),
            ]
            + [pl.BlockSpec((1, NP, NC, 1, SEG, CQ, KF), source_map(k)) for k in range(K)],
            out_specs=pl.BlockSpec((NX, 1, NC, K * CQ, SLOTS * R_CH), lambda o, info: (0, o, 0, 0, 0)),
        ),
        out_shape=jax.ShapeDtypeStruct((NX, NY, NC, K * CQ, SLOTS * R_CH), BF),
        compiler_params=pltpu.CompilerParams(vmem_limit_bytes=VMEM),
        name="correlate",
    )(info, kernels, lags, *([gathered] * K))


def finish_body(parts_ref, out_ref):
    pieces = []
    for p in range(NP):
        for c in range(NC):
            for y in range(NY):
                total = parts_ref[(p * NY + y) * NC + c].astype(F32)
                for x in range(1, NO):
                    total = total + parts_ref[((x * NP + p) * NY + y) * NC + c].astype(F32)
                pieces.append(total)
    for k in range(K):
        rows = jnp.concatenate([v[k * CQ : (k + 1) * CQ] for v in pieces], axis=0).T.astype(BF)
        for q in range(SLOTS):
            out_ref[0, q, k] = rows[q * R_CH : (q + 1) * R_CH]


def finish(parts):
    return pl.pallas_call(
        finish_body,
        out_shape=jax.ShapeDtypeStruct((1, SLOTS, K, R_CH, CH), BF),
        compiler_params=pltpu.CompilerParams(vmem_limit_bytes=VMEM),
        name="finish",
    )(parts)


def body(traces, source_list, source_count, receiver_start, segment_slot):
    y = lax.axis_index("y")
    z = lax.axis_index("z")
    table = jnp.asarray(transform_table())
    lags = jnp.asarray(lag_tables())
    split, low, high = whiten(traces, table)
    crossed = lax.all_to_all(split, ("xl", "c", "y"), 0, 0).reshape(NP, NC, NY, SEG, CQ, KF)
    gathered = lax.all_gather(crossed, "z", axis=0, tiled=False)

    low, high, _ = lax.optimization_barrier((low, high, crossed))
    pairs = NY * NZ
    following = lax.ppermute(low, ("y", "z"), [(p, p - 1) for p in range(1, pairs)])
    joined = jnp.concatenate([high, following], axis=1)
    offset = lax.dynamic_index_in_dim(receiver_start, y * NZ + z, keepdims=False) - CH // 2
    window = lax.dynamic_slice_in_dim(joined, offset, R_CH, 1)
    own = jnp.stack(
        [window] + [lax.ppermute(window, "y", [(i, (i + d) % NY) for i in range(NY)]) for d in range(1, NY)]
    )
    other = lax.ppermute(own, "c", [(0, 1), (1, 0)])
    chip = jnp.concatenate([own, other], axis=1)
    beside = lax.ppermute(chip, "xl", [(0, 1), (1, 0)])
    core = jnp.stack([lax.axis_index("c"), lax.axis_index("xl")]).astype(jnp.int32)
    kernels = lag_kernels(core, chip, lags, 0, None)
    kernels = lag_kernels(core, beside, lags, SEG * NC, kernels)

    lists = lax.dynamic_index_in_dim(source_list.reshape(NY, NZ, K), z, 1, keepdims=False).reshape(-1)
    counts = lax.dynamic_index_in_dim(source_count.reshape(NY, NZ), z, 1, keepdims=False)
    rows = list(lists.reshape(NY, K))
    for o in range(1, NY):
        rows[o] = jnp.where(jnp.arange(K, dtype=jnp.int32) < counts[o], rows[o], rows[o - 1])
    lists = jnp.concatenate(rows)
    slots = lax.dynamic_slice_in_dim(segment_slot, lax.axis_index("xh") * SEG_PAIR, SEG_PAIR, 0)
    info = jnp.concatenate([lists % NZ, lists // NZ, counts, slots, y[None].astype(jnp.int32)])
    sums = correlate(info, kernels, lags, gathered)
    parts = lax.all_to_all(sums.reshape(NY * LAGS, K * CQ, SLOTS * R_CH), ("xh", "xl", "y", "c"), 0, 0)
    return finish(parts)


def solution(mesh):
    grid = Mesh(mesh.devices.reshape(NY, NZ, NO, NP, NC), ("y", "z", "xh", "xl", "c"))
    tm, pair = ("xh", "xl", "c"), ("y", "z")
    return jax.shard_map(
        body,
        mesh=grid,
        in_specs=(P(tm, None, pair), P(), P(), P(), P()),
        out_specs=P(tm, None, pair, None, None),
        check_vma=False,
    )
```
